128 devices in a mesh: lon: 32 (over x, y, z_lo), dep: 4 (over z_hi, core).
Axes of the slice: x: 4, y: 4, z: 4 (z_hi: 2, z_lo: 2; z = z_hi * 2 + z_lo), core: 2. Of those that a mesh axis runs over, the one named last changes fastest.
Arguments:
- tracers: float32 [2, 80, 64, 4096], P(None, 'dep', None, 'lon'), may hold values from -6 to 6
- u_east: float32 [80, 64, 4096], P('dep', None, 'lon'), may hold values from -0.24 to 0.24
- v_north: float32 [80, 64, 4096], P('dep', None, 'lon'), may hold values from -0.24 to 0.24
- kappa_h: float32 [80, 64, 4096], P('dep', None, 'lon'), may hold values from 0.05 to 0.25
- kappa_v: float32 [80, 64, 4096], P('dep', None, 'lon'), may hold values from 0.3 to 300
- bottom: int32 [64, 4096], P(None, 'lon'), may hold values from 0 to 80
Outputs:
- tracers_out: float32 [2, 80, 64, 4096], P(None, 'dep', None, 'lon')
The draws below stay inside these ranges and needn't reach their ends.
Inputs may be any that keep to these rules, and one draw needn't show every extreme that they name: Levels from bottom down are land; a column with 0 is all land.
All inputs are finite; a program needn't handle non-finite values.
Results may differ from the reference program's by a relative error of at most 0.0003.
Values sent between devices are 32-bit elements; how exact they have to be, the bound alone decides.
A program may use at most 128 MiB of HBM per device.

```python
import math
import jax
import jax.numpy as jnp
from jax import lax

LAT = 64
SUB = 4
NLON = 4096
NLEV = 80


def with_ends(drawn, key, low, largest):
    dims = drawn.shape
    place = [jax.random.randint(jax.random.fold_in(key, axis), (), 0, dims[axis]) for axis in range(len(dims))]
    drawn = drawn.at[tuple(place)].set(low)
    longest = dims.index(max(dims))
    place[longest] = (place[longest] + 1) % dims[longest]
    return drawn.at[tuple(place)].set(largest)


def block_scale(stream_key, dims, cuts, least, largest):
    gain = 1.0
    for axis_at, blocks in cuts:
        steps = jax.random.uniform(jax.random.fold_in(jax.random.fold_in(stream_key, 6), axis_at), (blocks,), jnp.float32, least / len(cuts), largest / len(cuts))
        gain = gain * jnp.repeat(jnp.exp(steps), dims[axis_at] // blocks).reshape((-1,) + (1,) * (len(dims) - 1 - axis_at))
    return gain


def centred(key, extent, width, reach, split=(), kind=jnp.bfloat16):
    loudness = block_scale(key, extent, split, -0.22, 0.18) if split else 1.0
    values = jax.random.normal(key, extent, jnp.float32) * width * loudness
    return jnp.minimum(jnp.maximum(values, -reach), reach).astype(kind)


def setup_inputs(seed: int = 0) -> dict:
    seeds = jax.random.split(jax.random.key(seed), 7)
    return {
        "tracers": centred(seeds[0], (2, NLEV, LAT, NLON), 1.0, 6.0, ((1, 4), (3, 32)), jnp.float32),
        "u_east": jnp.clip(jax.random.uniform(seeds[1], (NLEV, LAT, NLON), jnp.float32, -0.24, 0.24) * block_scale(seeds[1], (NLEV, LAT, NLON), ((0, 4), (2, 32)), -0.4, 0.0), -0.24, 0.24),
        "v_north": jnp.clip(jax.random.uniform(seeds[2], (NLEV, LAT, NLON), jnp.float32, -0.24, 0.24) * block_scale(seeds[2], (NLEV, LAT, NLON), ((0, 4), (2, 32)), -0.4, 0.0), -0.24, 0.24),
        "kappa_h": jnp.clip(jnp.exp(math.log(0.25) - 1.609438 * jax.random.uniform(seeds[3], (NLEV, LAT, NLON), jnp.float32) ** block_scale(seeds[3], (NLEV, LAT, NLON), ((0, 4), (2, 32)), -0.2, 0.2)), 0.05, 0.25),
        "kappa_v": jnp.clip(jnp.exp(math.log(300.0) - 6.9077552 * jax.random.uniform(seeds[4], (NLEV, LAT, NLON), jnp.float32) ** block_scale(seeds[4], (NLEV, LAT, NLON), ((0, 4), (2, 32)), -0.2, 0.2)), 0.3, 300.0),
        "bottom": with_ends(jax.random.randint(seeds[5], (LAT, NLON), 0, NLEV + 1), jax.random.fold_in(seeds[5], 1), 0, NLEV).astype(jnp.int32),
    }


thermal_coef = 0.2
haline_coef = 0.8


def wrap_lon(field, margin):
    return jnp.concatenate([field[..., -margin:], field, field[..., :margin]], axis=-1)


def shift_north(field):
    return jnp.concatenate([field[..., 1:, :], jnp.zeros_like(field[..., :1, :])], axis=-2)


def shift_south(field):
    return jnp.concatenate([jnp.zeros_like(field[..., :1, :]), field[..., :-1, :]], axis=-2)


def upwind_step(tracer_ext, zonal_ext, merid_mid, wet_ext):
    face_wet = wet_ext[..., :-1] * wet_ext[..., 1:]
    zonal_face = zonal_ext[..., :-1]
    flux_all = face_wet * (jnp.maximum(zonal_face, 0.0) * tracer_ext[..., :-1] + jnp.minimum(zonal_face, 0.0) * tracer_ext[..., 1:])
    flux_east = flux_all[..., 1:]
    flux_west = flux_all[..., :-1]
    middle = tracer_ext[..., 1:-1]
    wet_mid = wet_ext[..., 1:-1]
    wet_north = wet_mid * shift_north(wet_mid)
    flux_north = wet_north * (jnp.maximum(merid_mid, 0.0) * middle + jnp.minimum(merid_mid, 0.0) * shift_north(middle))
    return middle - (flux_east - flux_west) - (flux_north - shift_south(flux_north))


def lon_diff(field):
    return 0.5 * (field[..., 2:] - field[..., :-2])


def lev_diff(field):
    return 0.5 * (field[..., 2:, :, :] - field[..., :-2, :, :])


def lat_diff(field):
    padded = jnp.concatenate([jnp.zeros_like(field[..., :1, :]), field, jnp.zeros_like(field[..., :1, :])], axis=-2)
    return 0.5 * (padded[..., 2:, :] - padded[..., :-2, :])


def isoneutral(tracer_ext, kappa_ext, wet_ext):
    mask_x = wet_ext[1:-1, :, 2:] * wet_ext[1:-1, :, :-2]
    mask_z = wet_ext[2:, :, 1:-1] * wet_ext[:-2, :, 1:-1]
    wet_pad = jnp.concatenate([jnp.zeros_like(wet_ext[:, :1, :]), wet_ext, jnp.zeros_like(wet_ext[:, :1, :])], axis=1)
    mask_y = (wet_pad[:, 2:, :] * wet_pad[:, :-2, :])[1:-1, :, 1:-1]
    grad_x = lon_diff(tracer_ext)[:, 1:-1] * mask_x
    grad_y = lat_diff(tracer_ext)[:, 1:-1, :, 1:-1] * mask_y
    grad_z = lev_diff(tracer_ext)[..., 1:-1] * mask_z
    dens_x = -thermal_coef * grad_x[0] + haline_coef * grad_x[1]
    dens_y = -thermal_coef * grad_y[0] + haline_coef * grad_y[1]
    dens_z = -thermal_coef * grad_z[0] + haline_coef * grad_z[1]
    denominator = 1.0 + dens_x * dens_x + dens_y * dens_y + dens_z * dens_z
    slope_x = dens_x * dens_z / denominator
    slope_y = dens_y * dens_z / denominator
    kappa_mid = kappa_ext[1:-1, :, 1:-1] * wet_ext[1:-1, :, 1:-1]
    flux_x = kappa_mid * (grad_x + slope_x * grad_z)
    flux_y = kappa_mid * (grad_y + slope_y * grad_z)
    flux_z = kappa_mid * (slope_x * grad_x + slope_y * grad_y + (slope_x * slope_x + slope_y * slope_y) * grad_z)
    tendency = lon_diff(flux_x)[:, 1:-1] + lat_diff(flux_y)[:, 1:-1, :, 1:-1] + lev_diff(flux_z)[..., 1:-1]
    return tracer_ext[:, 2:-2, :, 2:-2] + tendency * wet_ext[2:-2, :, 2:-2]


def forward_sweep(right_side, e_top, e_low, start_ratio, start_value):
    def advance(carry, level):
        ratio, value = carry
        source_k, top_k, low_k = level
        denominator = 1.0 + top_k + low_k + top_k * ratio
        new_ratio = -low_k / denominator
        new_value = (source_k + top_k * value) / denominator
        return (new_ratio, new_value), (new_ratio, new_value)
    return lax.scan(advance, (start_ratio, start_value), (right_side, e_top, e_low))


def back_sweep(ratios, values, start):
    def advance(below, level):
        ratio, value = level
        here = value - ratio * below
        return here, here
    _, result = lax.scan(advance, start, (ratios, values), reverse=True)
    return result


def column_solve(tracer, e_top):
    e_low = jnp.concatenate([e_top[1:], jnp.zeros_like(e_top[:1])], axis=0)
    right_side = jnp.moveaxis(tracer, 1, 0)
    start_ratio = jnp.zeros(e_top.shape[1:], jnp.float32)
    start_value = jnp.zeros(right_side.shape[1:], jnp.float32)
    _, (ratios, values) = forward_sweep(right_side, e_top, e_low, start_ratio, start_value)
    result = back_sweep(ratios, values, start_value)
    return jnp.moveaxis(result, 0, 1)


def reference(tracers, u_east, v_north, kappa_h, kappa_v, bottom):
    level_ids = jnp.arange(NLEV, dtype=jnp.int32)[:, None, None]
    wet = (level_ids < bottom[None]).astype(jnp.float32)
    tracer_now = tracers
    wet_cycle = wrap_lon(wet, 1)
    zonal_cycle = wrap_lon(u_east, 1)
    for substep in range(SUB):
        tracer_now = upwind_step(wrap_lon(tracer_now, 1), zonal_cycle, v_north, wet_cycle)
    tracer_ext = jnp.pad(wrap_lon(tracer_now, 2), ((0, 0), (2, 2), (0, 0), (0, 0)))
    kappa_ext = jnp.pad(wrap_lon(kappa_h, 2), ((2, 2), (0, 0), (0, 0)))
    wet_ext = jnp.pad(wrap_lon(wet, 2), ((2, 2), (0, 0), (0, 0)))
    tracer_now = isoneutral(tracer_ext, kappa_ext, wet_ext)
    e_top = kappa_v * ((level_ids >= 1) & (level_ids < bottom[None])).astype(jnp.float32)
    return column_solve(tracer_now, e_top)
```

```python
import functools

import jax
import jax.numpy as jnp
from jax import lax
from jax.experimental import pallas as pl
from jax.experimental.pallas import tpu as pltpu
from jax.sharding import PartitionSpec as P

MESH = pl.DeviceIdType.MESH
SUB = 4
LAT = 64
LON = 128
THERMAL = 0.2
HALINE = 0.8
FAR = 1 << 20

(LON_R, LON_L, BOT_R, BOT_L, DG_RU, DG_RD, DG_LU, DG_LD, E_U, E_D, K_U, K_D, KX_U, KX_D, KV_U, ADV_U, ADV_D, ZM, QM, ZV, YV, XO) = range(22)
N_COPIES = 22


def lanes(shape):
    return lax.broadcasted_iota(jnp.int32, shape, len(shape) - 1)


def rows(shape):
    return lax.broadcasted_iota(jnp.int32, shape, len(shape) - 2)


def plane_shifts():
    def east(x):
        return pltpu.roll(x, LON - 1, x.ndim - 1)

    def west(x):
        return pltpu.roll(x, 1, x.ndim - 1)

    def north(x):
        return pltpu.roll(x, LAT - 1, x.ndim - 2)

    def south(x):
        return pltpu.roll(x, 1, x.ndim - 2)

    return east, west, north, south


def strip_shifts():
    def east(x):
        return pltpu.roll(x, LON - 1, x.ndim - 1)

    def west(x):
        return pltpu.roll(x, 1, x.ndim - 1)

    def north(x):
        y = pltpu.roll(x, 7, x.ndim - 2)
        return jnp.where(rows(x.shape) == 7, pltpu.roll(y, 112, x.ndim - 1), y)

    def south(x):
        y = pltpu.roll(x, 1, x.ndim - 2)
        return jnp.where(rows(x.shape) == 0, pltpu.roll(y, 16, x.ndim - 1), y)

    return east, west, north, south


def is_first_row(shape, strip):
    if strip:
        return (rows(shape) == 0) & (lanes(shape) < 16)
    return rows(shape) == 0


def is_last_row(shape, strip):
    if strip:
        return (rows(shape) == 7) & (lanes(shape) >= 112)
    return rows(shape) == LAT - 1


def upwind(c0, c1, u, v, face_x, face_y, shifts):
    east, west, north, south = shifts
    u = jnp.where(face_x, u, 0.0)
    v = jnp.where(face_y, v, 0.0)
    up = jnp.maximum(u, 0.0)
    vp = jnp.maximum(v, 0.0)
    ce = up - u
    cn = vp - v
    cw = west(up)
    cs = south(vp)
    keep = 1.0 - up - vp - west(ce) - south(cn)

    def advance(c):
        return keep * c + cw * west(c) + ce * east(c) + cs * south(c) + cn * north(c)

    for _ in range(SUB):
        c0 = advance(c0)
        c1 = advance(c1)
    return c0, c1


def fluxes(low, mid, high, kappa, mask_x, mask_y, mask_z, shifts):
    east, west, north, south = shifts
    gx = [jnp.where(mask_x, east(c) - west(c), 0.0) for c in mid]
    gy = [jnp.where(mask_y, north(c) - south(c), 0.0) for c in mid]
    gz = [jnp.where(mask_z, h - l, 0.0) for l, h in zip(low, high)]

    def density(g):
        return (-0.5 * THERMAL) * g[0] + (0.5 * HALINE) * g[1]

    rx, ry, rz = density(gx), density(gy), density(gz)
    ratio = rz / (1.0 + rx * rx + ry * ry + rz * rz)
    sx, sy = rx * ratio, ry * ratio
    sq = sx * sx + sy * sy
    flat, vert = [], []
    for n in range(2):
        fx = kappa * (gx[n] + sx * gz[n])
        fy = kappa * (gy[n] + sy * gz[n])
        vert.append(kappa * (sx * gx[n] + sy * gy[n] + sq * gz[n]))
        flat.append((east(fx) - west(fx)) + (north(fy) - south(fy)))
    return flat, vert


def pack(tiles, offset):
    group = lanes(tiles[0].shape) // 16
    out = None
    for g in range(8):
        moved = pltpu.roll(tiles[g], (16 * g + offset) % LON, tiles[g].ndim - 1)
        out = moved if out is None else jnp.where(group == g, moved, out)
    return out


def tiles_of(plane):
    return [plane[..., 8 * g : 8 * g + 8, :] for g in range(8)]


def kernel(
    n_lon, n_dep, n_lev,
    tr_hbm, u_hbm, v_hbm, kh_hbm, kv_hbm, bot_hbm,
    out_hbm,
    tr, u, v, kx, kv, bot,
    bmask, bstrip, bown, brecv,
    eown, kown, msg_r, msg_l, from_l, from_r,
    adv, flat, vert, gwin, awin, sflat, svert, edge,
    inv, gdn, rdn, rprod, pspk, qspk, fval, yend, send_end,
    zmat, qmat, qpart, zval, yval, ypart, xout, xend, tmat,
    obuf, in_sem, out_sem, ssem, rsem,
):
    lon = lax.axis_index("lon")
    dep = lax.axis_index("dep")
    right = lax.rem(lon + 1, n_lon)
    left = lax.rem(lon + n_lon - 1, n_lon)
    first = dep * n_lev
    has_up = dep > 0
    has_dn = dep < n_dep - 1
    inner = (dep == 1) | (dep == 2)
    outer = jnp.logical_not(inner)
    o_end = jnp.where(dep < 2, 0, 1)
    i_end = 1 - o_end
    out_dev = jnp.where(dep < 2, 0, 3)
    in_dev = jnp.where(dep < 2, 1, 2)
    plane = (LAT, LON)
    tile = (8, LON)

    def remote(src, dst, index, device):
        return pltpu.make_async_remote_copy(
            src_ref=src, dst_ref=dst, send_sem=ssem.at[index], recv_sem=rsem.at[index],
            device_id=device, device_id_type=MESH,
        )

    loads = [
        pltpu.make_async_copy(bot_hbm, bot, in_sem.at[0]),
        pltpu.make_async_copy(tr_hbm, tr, in_sem.at[1]),
        pltpu.make_async_copy(u_hbm, u, in_sem.at[2]),
        pltpu.make_async_copy(v_hbm, v, in_sem.at[3]),
        pltpu.make_async_copy(kh_hbm, kx.at[pl.ds(1, n_lev)], in_sem.at[4]),
        pltpu.make_async_copy(kv_hbm, kv.at[pl.ds(0, n_lev)], in_sem.at[5]),
    ]
    for copy in loads:
        copy.start()

    barrier = pltpu.get_barrier_semaphore()

    def greet(device):
        pl.semaphore_signal(barrier, inc=1, device_id=device, device_id_type=MESH)

    greet((right, dep))
    greet((left, dep))

    @pl.when(has_up)
    def _():
        greet((lon, dep - 1))
        greet((right, dep - 1))
        greet((left, dep - 1))

    @pl.when(has_dn)
    def _():
        greet((lon, dep + 1))
        greet((right, dep + 1))
        greet((left, dep + 1))

    def clear(ref, start, count):
        part = ref.at[pl.ds(start, count)]
        part[...] = jnp.zeros(part.shape, part.dtype)

    @pl.when(jnp.logical_not(has_up))
    def _():
        clear(from_l, 0, 2)
        clear(from_r, 0, 2)
        clear(eown, 0, 2)
        clear(kown, 0, 1)
        clear(kx, 0, 1)
        clear(adv, 0, 2)

    @pl.when(jnp.logical_not(has_dn))
    def _():
        clear(from_l, n_lev + 2, 2)
        clear(from_r, n_lev + 2, 2)
        clear(eown, n_lev + 2, 2)
        clear(kown, n_lev + 1, 1)
        clear(kx, n_lev + 1, 1)
        clear(adv, n_lev + 2, 2)
        clear(kv, n_lev, 1)

    clear(kown, n_lev + 2, 2)
    clear(awin, n_lev + 4, 2)

    lo8 = lanes(tile) % 16 < 8

    loads[0].wait()
    b = bot[...]
    bown[0] = pack(tiles_of(b), 8)
    bown[1] = pack(tiles_of(b), 4)
    bown[2] = pack(tiles_of(b), 12)

    def edge_masks(b, shifts, strip):
        east, west, north, south = shifts
        top = is_first_row(b.shape, strip)
        end = is_last_row(b.shape, strip)
        bn = jnp.where(end, 0, north(b))
        bs = jnp.where(top, 0, south(b))
        be, bw = east(b), west(b)
        return b, jnp.minimum(b, be), jnp.minimum(b, bn), jnp.minimum(bw, be), jnp.minimum(bs, bn)

    for i, value in enumerate(edge_masks(b, plane_shifts(), False)):
        bmask[i] = value

    for copy in loads[1:5]:
        copy.wait()
    chunk = 4
    shape = (chunk, 8, LON)

    def pack_levels(step, carry):
        at = step * chunk
        low = lanes(shape) % 16 < 8
        wl = lanes(shape) % 16

        def field(ref, offset):
            return pack([ref[pl.ds(at, chunk), 8 * g : 8 * g + 8, :] for g in range(8)], offset)

        t, s = field(tr.at[0], 8), field(tr.at[1], 8)
        uu, vv = field(u, 8), field(v, 8)
        kref = kx.at[pl.ds(1, n_lev)]
        kl, kr = field(kref, 4), field(kref, 12)
        eown[pl.ds(at + 2, chunk), 0] = t
        eown[pl.ds(at + 2, chunk), 1] = s
        eown[pl.ds(at + 2, chunk), 2] = uu
        eown[pl.ds(at + 2, chunk), 3] = vv
        kown[pl.ds(at + 1, chunk), 0] = kl
        kown[pl.ds(at + 1, chunk), 1] = kr
        msg_r[pl.ds(at, chunk), 0] = jnp.where(low, t, pltpu.roll(s, 8, 2))
        msg_r[pl.ds(at, chunk), 1] = jnp.where(
            wl == 8, pltpu.roll(kr, LON - 3, 2), jnp.where(low, uu, pltpu.roll(vv, 8, 2))
        )
        msg_l[pl.ds(at, chunk), 0] = jnp.where(low, pltpu.roll(s, LON - 8, 2), t)
        msg_l[pl.ds(at, chunk), 1] = jnp.where(
            wl == 7, pltpu.roll(kl, 3, 2), jnp.where(low, pltpu.roll(vv, LON - 8, 2), uu)
        )
        return carry

    lax.fori_loop(0, n_lev // chunk, pack_levels, 0)
    loads[5].wait()

    @pl.when(has_up & has_dn)
    def _():
        pl.semaphore_wait(barrier, 8)

    @pl.when(jnp.logical_not(has_up & has_dn))
    def _():
        pl.semaphore_wait(barrier, 5)

    top2, end2 = pl.ds(0, 2), pl.ds(n_lev - 2, 2)
    pre2, post2 = pl.ds(0, 2), pl.ds(n_lev + 2, 2)
    lon_r = remote(msg_r, from_l.at[pl.ds(2, n_lev)], LON_R, (right, dep))
    lon_l = remote(msg_l, from_r.at[pl.ds(2, n_lev)], LON_L, (left, dep))
    bot_r = remote(bown.at[0], brecv.at[0], BOT_R, (right, dep))
    bot_l = remote(bown.at[0], brecv.at[1], BOT_L, (left, dep))
    ups = [
        remote(msg_r.at[top2], from_l.at[post2], DG_RU, (right, dep - 1)),
        remote(msg_l.at[top2], from_r.at[post2], DG_LU, (left, dep - 1)),
        remote(eown.at[pl.ds(2, 2)], eown.at[post2], E_U, (lon, dep - 1)),
        remote(kown.at[1], kown.at[n_lev + 1], K_U, (lon, dep - 1)),
        remote(kx.at[1], kx.at[n_lev + 1], KX_U, (lon, dep - 1)),
        remote(kv.at[0], kv.at[n_lev], KV_U, (lon, dep - 1)),
        remote(adv.at[pl.ds(2, 2)], adv.at[post2], ADV_U, (lon, dep - 1)),
    ]
    downs = [
        remote(msg_r.at[end2], from_l.at[pre2], DG_RD, (right, dep + 1)),
        remote(msg_l.at[end2], from_r.at[pre2], DG_LD, (left, dep + 1)),
        remote(eown.at[pl.ds(n_lev, 2)], eown.at[pre2], E_D, (lon, dep + 1)),
        remote(kown.at[n_lev], kown.at[0], K_D, (lon, dep + 1)),
        remote(kx.at[n_lev], kx.at[0], KX_D, (lon, dep + 1)),
        remote(adv.at[pl.ds(n_lev, 2)], adv.at[pre2], ADV_D, (lon, dep + 1)),
    ]
    bot_r.start()
    bot_l.start()

    @pl.when(has_up)
    def _():
        for copy in ups[:-1]:
            copy.start()

    @pl.when(has_dn)
    def _():
        for copy in downs[:-1]:
            copy.start()

    lon_r.start()
    lon_l.start()

    def transport(at):
        k = first + at
        c0, c1 = upwind(
            tr[0, at], tr[1, at], u[at], v[at], bmask[1] > k, bmask[2] > k, plane_shifts()
        )
        adv[at + 2, 0] = c0
        adv[at + 2, 1] = c1

    def transport_ends(step, carry):
        transport(jnp.where(step < 2, step, step + n_lev - 4))
        return carry

    def transport_rest(step, carry):
        transport(step)
        return carry

    lax.fori_loop(0, 4, transport_ends, 0)

    @pl.when(has_up)
    def _():
        ups[-1].start()

    @pl.when(has_dn)
    def _():
        downs[-1].start()

    @pl.when(has_dn)
    def _():
        ups[5].wait_recv()

    def e_of(at):
        k = first + at
        k = jnp.where(k < 1, FAR, k)
        return jnp.where(bmask[0] > k, kv[at], 0.0)

    def eliminate(at, carry):
        ratio, prod, spike, p_top, e_here = carry
        e_next = e_of(at + 1)
        recip = 1.0 / (1.0 + e_next + e_here * (1.0 - ratio))
        gain = e_here * recip
        inv[at] = recip
        gdn[at] = gain
        rprod[at] = prod
        ratio = e_next * recip
        rdn[at] = ratio
        spike = spike * gain
        pspk[at] = spike
        p_top = p_top + prod * spike
        return ratio, prod * ratio, spike, p_top, e_next

    zero, one = jnp.zeros(plane, jnp.float32), jnp.ones(plane, jnp.float32)
    _, q_top, p_end, p_top, _ = lax.fori_loop(
        0, n_lev, eliminate, (zero, one, one, zero, e_of(0))
    )
    send_end[0, 0] = p_top
    send_end[0, 1] = p_end
    send_end[1, 0] = q_top
    send_end[1, 1] = rdn[n_lev - 1]
    z_copy = remote(send_end.at[i_end, i_end], zmat, ZM, (lon, in_dev))
    q_copy = remote(qmat, qpart, QM, (lon, 3 - dep))

    @pl.when(outer)
    def _():
        z_copy.start()

    def back_matrix(step, carry):
        p_low, q_low = carry
        at = n_lev - 1 - step
        ratio = rdn[at]
        p = pspk[at] + ratio * p_low
        q = ratio * q_low
        pspk[at] = p
        qspk[at] = q
        return p, q

    lax.fori_loop(0, n_lev, back_matrix, (zero, one))

    lax.fori_loop(2, n_lev - 2, transport_rest, 0)

    @pl.when(inner)
    def _():
        z_copy.wait_recv()
        z = zmat[...]
        inv_t = 1.0 / (1.0 - z * send_end[o_end, o_end])
        tmat[0] = inv_t
        beta = z * send_end[i_end, o_end] * inv_t
        tmat[1] = beta
        qmat[...] = send_end[i_end, i_end] + send_end[o_end, i_end] * beta
        q_copy.start()

    def flux_level(at):
        k = first + at - 1
        kw = jnp.where(k < 0, FAR, k)
        kz = jnp.where(k < 1, FAR, k + 1)
        kappa = jnp.where(bmask[0] > kw, 0.25 * kx[at], 0.0)
        f, w = fluxes(
            [adv[at, n] for n in range(2)], [adv[at + 1, n] for n in range(2)],
            [adv[at + 2, n] for n in range(2)], kappa,
            bmask[3] > kw, bmask[4] > kw, bmask[0] > kz, plane_shifts(),
        )
        for n in range(2):
            flat[at, n] = f[n]
            vert[at, n] = w[n]

    def flux_rest(step, carry):
        flux_level(step)
        return carry

    def flux_ends(step, carry):
        flux_level(jnp.where(step < 2, step, step + n_lev - 2))
        return carry

    lax.fori_loop(2, n_lev, flux_rest, 0)

    @pl.when(has_dn)
    def _():
        ups[4].wait_recv()
        ups[6].wait_recv()

    @pl.when(has_up)
    def _():
        downs[4].wait_recv()
        downs[5].wait_recv()

    lax.fori_loop(0, 4, flux_ends, 0)

    def pack_windows(step, carry):
        at = step * chunk
        low = lanes(shape) % 16 < 8
        for n in range(2):
            parts = [adv[pl.ds(at, chunk), n, 8 * g : 8 * g + 8, :] for g in range(8)]
            gwin[n, pl.ds(at, chunk)] = jnp.where(low, pack(parts, 12), pack(parts, 4))
        return carry

    lax.fori_loop(0, (n_lev + 4) // chunk, pack_windows, 0)

    bot_r.wait_recv()
    bot_l.wait_recv()
    lon_r.wait_recv()
    lon_l.wait_recv()

    @pl.when(has_dn)
    def _():
        for copy in ups[:4]:
            copy.wait_recv()

    @pl.when(has_up)
    def _():
        for copy in downs[:4]:
            copy.wait_recv()

    b_l = jnp.where(lo8, brecv[0], bown[0])
    b_r = jnp.where(lo8, bown[0], brecv[1])
    w_l = jnp.where(lo8, pltpu.roll(b_l, LON - 4, 1), bown[1])
    w_r = jnp.where(lo8, bown[2], pltpu.roll(b_r, 4, 1))
    for side, value in enumerate((b_l, b_r)):
        masks = edge_masks(value, strip_shifts(), True)
        bstrip[0, side] = masks[1]
        bstrip[1, side] = masks[2]
    for side, value in enumerate((w_l, w_r)):
        masks = edge_masks(value, strip_shifts(), True)
        bstrip[2, side] = masks[0]
        bstrip[3, side] = masks[3]
        bstrip[4, side] = masks[4]

    flatshape = (2 * chunk, 8, LON)

    def level_mask(which, start, floor, shift):
        parts = []
        for i in range(chunk):
            k = start + i
            k = jnp.where(k < floor, FAR, k + shift)
            parts.append(bstrip[which] > k)
        return jnp.concatenate(parts, axis=0)

    def join(left_part, right_part):
        return jnp.stack([left_part, right_part], axis=1).reshape(flatshape)

    def strip_transport(step, carry):
        at = step * chunk
        k = first + at - 2
        low = lanes(shape) % 16 < 8
        own = [eown[pl.ds(at, chunk), i] for i in range(4)]
        la, lb = from_l[pl.ds(at, chunk), 0], from_l[pl.ds(at, chunk), 1]
        ra, rb = from_r[pl.ds(at, chunk), 0], from_r[pl.ds(at, chunk), 1]

        def assemble(i, from_left, from_right):
            return join(jnp.where(low, from_left, own[i]), jnp.where(low, own[i], from_right))

        c0 = assemble(0, la, ra)
        c1 = assemble(1, pltpu.roll(la, LON - 8, 2), pltpu.roll(ra, 8, 2))
        uu = assemble(2, lb, rb)
        vv = assemble(3, pltpu.roll(lb, LON - 8, 2), pltpu.roll(rb, 8, 2))
        done = upwind(c0, c1, uu, vv, level_mask(0, k, 0, 0), level_mask(1, k, 0, 0), strip_shifts())
        for n in range(2):
            both = done[n].reshape(chunk, 2, 8, LON)
            g = gwin[n, pl.ds(at, chunk)]
            awin[pl.ds(at, chunk), n, 0] = jnp.where(low, pltpu.roll(both[:, 0], LON - 4, 2), g)
            awin[pl.ds(at, chunk), n, 1] = jnp.where(low, g, pltpu.roll(both[:, 1], 4, 2))
        return carry

    lax.fori_loop(0, (n_lev + 4) // chunk, strip_transport, 0)

    def strip_flux(step, carry):
        at = step * chunk
        k = first + at - 1
        wl = lanes(shape) % 16
        lb, rb = from_l[pl.ds(at + 1, chunk), 1], from_r[pl.ds(at + 1, chunk), 1]
        kl = jnp.where(wl == 3, pltpu.roll(lb, LON - 5, 2), kown[pl.ds(at, chunk), 0])
        kr = jnp.where(wl == 12, pltpu.roll(rb, 5, 2), kown[pl.ds(at, chunk), 1])
        kappa = jnp.where(level_mask(2, k, 0, 0), 0.25 * join(kl, kr), 0.0)

        def window(shift):
            return [awin[pl.ds(at + shift, chunk), n].reshape(flatshape) for n in range(2)]

        f, w = fluxes(
            window(0), window(1), window(2), kappa,
            level_mask(3, k, 0, 0), level_mask(4, k, 0, 0), level_mask(2, k, 1, 1), strip_shifts(),
        )
        for n in range(2):
            sflat[pl.ds(at, chunk), n] = f[n].reshape(chunk, 2, 8, LON)
            svert[pl.ds(at, chunk), n] = w[n].reshape(chunk, 2, 8, LON)
        return carry

    lax.fori_loop(0, (n_lev + 4) // chunk, strip_flux, 0)

    def strip_update(step, carry):
        at = step * chunk
        low = lanes(shape) % 16 < 8
        wet = level_mask(2, first + at, 0, 0)
        for n in range(2):
            gain = (
                sflat[pl.ds(at + 1, chunk), n] + svert[pl.ds(at + 2, chunk), n] - svert[pl.ds(at, chunk), n]
            ).reshape(flatshape)
            new = awin[pl.ds(at + 2, chunk), n].reshape(flatshape) + jnp.where(wet, gain, 0.0)
            both = new.reshape(chunk, 2, 8, LON)
            edge[pl.ds(at, chunk), n] = jnp.where(
                low, pltpu.roll(both[:, 1], LON - 4, 2), pltpu.roll(both[:, 0], 4, 2)
            )
        return carry

    lax.fori_loop(0, n_lev // chunk, strip_update, 0)

    yend[...] = jnp.zeros(yend.shape, jnp.float32)
    fval[0] = jnp.zeros((2,) + plane, jnp.float32)
    lane = lanes(plane)
    on_edge = (lane < 6) | (lane >= LON - 6)

    def way_down(at, carry):
        wet = bmask[0] > first + at
        scale, gain, prod = inv[at], gdn[at], rprod[at]
        for n in range(2):
            new = adv[at + 2, n] + jnp.where(wet, flat[at + 1, n] + vert[at + 2, n] - vert[at, n], 0.0)
            packed = edge[at, n]
            fixed = jnp.concatenate(
                [pltpu.roll(packed, (LON - 8 - 16 * g) % LON, 1) for g in range(8)], axis=0
            )
            new = jnp.where(on_edge, fixed, new)
            value = new * scale + gain * fval[at, n]
            fval[at + 1, n] = value
            yend[0, n] = yend[0, n] + prod * value
        return carry

    lax.fori_loop(0, n_lev, way_down, 0)
    yend[1] = fval[n_lev]

    z_val = remote(yend.at[i_end], zval, ZV, (lon, in_dev))
    y_val = remote(yval, ypart, YV, (lon, 3 - dep))
    x_val = remote(xout, xend.at[i_end], XO, (lon, out_dev))

    @pl.when(outer)
    def _():
        z_val.start()
        xend[o_end] = jnp.zeros((2,) + plane, jnp.float32)

    @pl.when(inner)
    def _():
        z_val.wait_recv()
        for n in range(2):
            alpha = (zval[n] + zmat[...] * yend[o_end, n]) * tmat[0]
            xend[o_end, n] = alpha
            yval[n] = yend[i_end, n] + send_end[o_end, i_end] * alpha
        y_val.start()

    def way_up(step, carry):
        at = n_lev - 1 - step
        ratio = rdn[at - 1]
        for n in range(2):
            fval[at, n] = fval[at, n] + ratio * fval[at + 1, n]
        return carry

    lax.fori_loop(0, n_lev - 1, way_up, 0)

    @pl.when(inner)
    def _():
        q_copy.wait_recv()
        y_val.wait_recv()
        q_other = qpart[...]
        inv_m = 1.0 / (1.0 - q_other * qmat[...])
        oo, io = send_end[o_end, o_end], send_end[i_end, o_end]
        for n in range(2):
            x_in = (ypart[n] + q_other * yval[n]) * inv_m
            xout[n] = (yend[o_end, n] + oo * zval[n] + io * x_in) * tmat[0]
            xend[i_end, n] = x_in
        x_val.start()
        for n in range(2):
            xend[o_end, n] = xend[o_end, n] + tmat[1] * xend[i_end, n]

    @pl.when(outer)
    def _():
        x_val.wait_recv()

    stores = []
    part = n_lev // 4
    for i in range(4):
        def finish(at, carry):
            p, q = pspk[at], qspk[at]
            for n in range(2):
                obuf[n, at] = fval[at + 1, n] + p * xend[0, n] + q * xend[1, n]
            return carry

        lax.fori_loop(i * part, (i + 1) * part, finish, 0)
        span = pl.ds(i * part, part)
        copy = pltpu.make_async_copy(obuf.at[:, span], out_hbm.at[:, span], out_sem.at[i])
        copy.start()
        stores.append(copy)

    for copy in (lon_r, lon_l, bot_r, bot_l):
        copy.wait_send()

    @pl.when(has_up)
    def _():
        for copy in ups:
            copy.wait_send()

    @pl.when(has_dn)
    def _():
        for copy in downs:
            copy.wait_send()

    @pl.when(outer)
    def _():
        z_copy.wait_send()
        z_val.wait_send()

    @pl.when(inner)
    def _():
        q_copy.wait_send()
        y_val.wait_send()
        x_val.wait_send()

    for copy in stores:
        copy.wait()


def per_device(n_lon, n_dep, tracers, u_east, v_north, kappa_h, kappa_v, bottom):
    n_lev = tracers.shape[1]
    ext = n_lev + 4

    def f32(*shape):
        return pltpu.VMEM(shape, jnp.float32)

    def i32(*shape):
        return pltpu.VMEM(shape, jnp.int32)

    scratch = [
        f32(2, n_lev, LAT, LON), f32(n_lev, LAT, LON), f32(n_lev, LAT, LON),
        f32(n_lev + 2, LAT, LON), f32(n_lev + 1, LAT, LON), i32(LAT, LON),
        i32(5, LAT, LON), i32(5, 2, 8, LON), i32(3, 8, LON), i32(2, 8, LON),
        f32(ext, 4, 8, LON), f32(ext, 2, 8, LON),
        f32(n_lev, 2, 8, LON), f32(n_lev, 2, 8, LON),
        f32(ext + 1, 2, 8, LON), f32(ext + 1, 2, 8, LON),
        f32(ext, 2, LAT, LON), f32(n_lev + 2, 2, LAT, LON), f32(n_lev + 2, 2, LAT, LON),
        f32(2, ext, 8, LON), f32(ext + 2, 2, 2, 8, LON),
        f32(ext, 2, 2, 8, LON), f32(ext, 2, 2, 8, LON), f32(n_lev, 2, 8, LON),
    ]
    scratch += [f32(n_lev, LAT, LON)] * 6
    scratch += [
        f32(n_lev + 1, 2, LAT, LON), f32(2, 2, LAT, LON), f32(2, 2, LAT, LON),
        f32(LAT, LON), f32(LAT, LON), f32(LAT, LON),
        f32(2, LAT, LON), f32(2, LAT, LON), f32(2, LAT, LON), f32(2, LAT, LON),
        f32(2, 2, LAT, LON), f32(2, LAT, LON),
        f32(2, n_lev, LAT, LON),
        pltpu.SemaphoreType.DMA((6,)), pltpu.SemaphoreType.DMA((4,)),
        pltpu.SemaphoreType.DMA((N_COPIES,)), pltpu.SemaphoreType.DMA((N_COPIES,)),
    ]
    hbm = pl.BlockSpec(memory_space=pl.ANY)
    return pl.pallas_call(
        functools.partial(kernel, n_lon, n_dep, n_lev),
        out_shape=jax.ShapeDtypeStruct(tracers.shape, jnp.float32),
        in_specs=[hbm] * 6,
        out_specs=hbm,
        scratch_shapes=scratch,
        name="tracer_step",
        compiler_params=pltpu.CompilerParams(
            collective_id=0, has_side_effects=True, vmem_limit_bytes=48 << 20
        ),
    )(tracers, u_east, v_north, kappa_h, kappa_v, bottom)


def solution(mesh):
    n_lon, n_dep = mesh.shape["lon"], mesh.shape["dep"]
    level = P("dep", None, "lon")
    return jax.shard_map(
        functools.partial(per_device, n_lon, n_dep),
        mesh=mesh,
        in_specs=(P(None, "dep", None, "lon"), level, level, level, level, P(None, "lon")),
        out_specs=P(None, "dep", None, "lon"),
        check_vma=False,
    )
```

```python
import functools

import jax
import jax.numpy as jnp
from jax import lax
from jax.experimental import pallas as pl
from jax.experimental.pallas import tpu as pltpu
from jax.sharding import PartitionSpec as P

MESH = pl.DeviceIdType.MESH
SUB = 4
LAT = 64
LON = 128
THERMAL = 0.2
HALINE = 0.8
FAR = 1 << 20

(LON_R, LON_L, BOT_R, BOT_L, DG_RU, DG_RD, DG_LU, DG_LD, E_U, E_D, K_U, K_D, KX_U, KX_D, KV_U, ADV_U, ADV_D, ZM, QM, ZV, YV, XO) = range(22)
N_COPIES = 22


def lanes(shape):
    return lax.broadcasted_iota(jnp.int32, shape, len(shape) - 1)


def rows(shape):
    return lax.broadcasted_iota(jnp.int32, shape, len(shape) - 2)


def plane_shifts():
    def east(x):
        return pltpu.roll(x, LON - 1, x.ndim - 1)

    def west(x):
        return pltpu.roll(x, 1, x.ndim - 1)

    def north(x):
        return pltpu.roll(x, LAT - 1, x.ndim - 2)

    def south(x):
        return pltpu.roll(x, 1, x.ndim - 2)

    return east, west, north, south


def strip_shifts():
    def east(x):
        return pltpu.roll(x, LON - 1, x.ndim - 1)

    def west(x):
        return pltpu.roll(x, 1, x.ndim - 1)

    def north(x):
        y = pltpu.roll(x, 7, x.ndim - 2)
        return jnp.where(rows(x.shape) == 7, pltpu.roll(y, 112, x.ndim - 1), y)

    def south(x):
        y = pltpu.roll(x, 1, x.ndim - 2)
        return jnp.where(rows(x.shape) == 0, pltpu.roll(y, 16, x.ndim - 1), y)

    return east, west, north, south


def is_first_row(shape, strip):
    if strip:
        return (rows(shape) == 0) & (lanes(shape) < 16)
    return rows(shape) == 0


def is_last_row(shape, strip):
    if strip:
        return (rows(shape) == 7) & (lanes(shape) >= 112)
    return rows(shape) == LAT - 1


def upwind(c0, c1, u, v, face_x, face_y, shifts):
    east, west, north, south = shifts
    u = jnp.where(face_x, u, 0.0)
    v = jnp.where(face_y, v, 0.0)
    up = jnp.maximum(u, 0.0)
    vp = jnp.maximum(v, 0.0)
    ce = up - u
    cn = vp - v
    cw = west(up)
    cs = south(vp)
    keep = 1.0 - up - vp - west(ce) - south(cn)

    def advance(c):
        return keep * c + cw * west(c) + ce * east(c) + cs * south(c) + cn * north(c)

    for _ in range(SUB):
        c0 = advance(c0)
        c1 = advance(c1)
    return c0, c1


def fluxes(low, mid, high, kappa, mask_x, mask_y, mask_z, shifts):
    east, west, north, south = shifts
    gx = [jnp.where(mask_x, east(c) - west(c), 0.0) for c in mid]
    gy = [jnp.where(mask_y, north(c) - south(c), 0.0) for c in mid]
    gz = [jnp.where(mask_z, h - l, 0.0) for l, h in zip(low, high)]

    def density(g):
        return (-0.5 * THERMAL) * g[0] + (0.5 * HALINE) * g[1]

    rx, ry, rz = density(gx), density(gy), density(gz)
    ratio = rz / (1.0 + rx * rx + ry * ry + rz * rz)
    sx, sy = rx * ratio, ry * ratio
    sq = sx * sx + sy * sy
    flat, vert = [], []
    for n in range(2):
        fx = kappa * (gx[n] + sx * gz[n])
        fy = kappa * (gy[n] + sy * gz[n])
        vert.append(kappa * (sx * gx[n] + sy * gy[n] + sq * gz[n]))
        flat.append((east(fx) - west(fx)) + (north(fy) - south(fy)))
    return flat, vert


def pack(tiles, offset):
    group = lanes(tiles[0].shape) // 16
    out = None
    for g in range(8):
        moved = pltpu.roll(tiles[g], (16 * g + offset) % LON, tiles[g].ndim - 1)
        out = moved if out is None else jnp.where(group == g, moved, out)
    return out


def tiles_of(plane):
    return [plane[..., 8 * g : 8 * g + 8, :] for g in range(8)]


def kernel(
    n_lon, n_dep, n_lev,
    tr_hbm, u_hbm, v_hbm, kh_hbm, kv_hbm, bot_hbm,
    out_hbm,
    tr, u, v, kx, kv, bot,
    bmask, bstrip, bown, brecv,
    eown, kown, msg_r, msg_l, from_l, from_r,
    adv, flat, vert, gwin, awin, sflat, svert, edge,
    inv, gdn, rdn, rprod, pspk, qspk, fval, yend, send_end,
    zmat, qmat, qpart, zval, yval, ypart, xout, xend, tmat,
    in_sem, ssem, rsem,
):
    lon = lax.axis_index("lon")
    dep = lax.axis_index("dep")
    right = lax.rem(lon + 1, n_lon)
    left = lax.rem(lon + n_lon - 1, n_lon)
    first = dep * n_lev
    has_up = dep > 0
    has_dn = dep < n_dep - 1
    inner = (dep == 1) | (dep == 2)
    outer = jnp.logical_not(inner)
    o_end = jnp.where(dep < 2, 0, 1)
    i_end = 1 - o_end
    out_dev = jnp.where(dep < 2, 0, 3)
    in_dev = jnp.where(dep < 2, 1, 2)
    plane = (LAT, LON)
    tile = (8, LON)

    def remote(src, dst, index, device):
        return pltpu.make_async_remote_copy(
            src_ref=src, dst_ref=dst, send_sem=ssem.at[index], recv_sem=rsem.at[index],
            device_id=device, device_id_type=MESH,
        )

    loads = [
        pltpu.make_async_copy(bot_hbm, bot, in_sem.at[0]),
        pltpu.make_async_copy(tr_hbm, tr, in_sem.at[1]),
        pltpu.make_async_copy(u_hbm, u, in_sem.at[2]),
        pltpu.make_async_copy(v_hbm, v, in_sem.at[3]),
        pltpu.make_async_copy(kh_hbm, kx.at[pl.ds(1, n_lev)], in_sem.at[4]),
        pltpu.make_async_copy(kv_hbm, kv.at[pl.ds(0, n_lev)], in_sem.at[5]),
    ]
    for copy in loads:
        copy.start()

    barrier = pltpu.get_barrier_semaphore()

    def greet(device):
        pl.semaphore_signal(barrier, inc=1, device_id=device, device_id_type=MESH)

    greet((right, dep))
    greet((left, dep))

    @pl.when(has_up)
    def _():
        greet((lon, dep - 1))
        greet((right, dep - 1))
        greet((left, dep - 1))

    @pl.when(has_dn)
    def _():
        greet((lon, dep + 1))
        greet((right, dep + 1))
        greet((left, dep + 1))

    def clear(ref, start, count):
        part = ref.at[pl.ds(start, count)]
        part[...] = jnp.zeros(part.shape, part.dtype)

    @pl.when(jnp.logical_not(has_up))
    def _():
        clear(from_l, 0, 2)
        clear(from_r, 0, 2)
        clear(eown, 0, 2)
        clear(kown, 0, 1)
        clear(kx, 0, 1)
        clear(adv, 0, 2)

    @pl.when(jnp.logical_not(has_dn))
    def _():
        clear(from_l, n_lev + 2, 2)
        clear(from_r, n_lev + 2, 2)
        clear(eown, n_lev + 2, 2)
        clear(kown, n_lev + 1, 1)
        clear(kx, n_lev + 1, 1)
        clear(adv, n_lev + 2, 2)
        clear(kv, n_lev, 1)

    clear(kown, n_lev + 2, 2)
    clear(awin, n_lev + 4, 2)

    lo8 = lanes(tile) % 16 < 8

    loads[0].wait()
    b = bot[...]
    bown[0] = pack(tiles_of(b), 8)
    bown[1] = pack(tiles_of(b), 4)
    bown[2] = pack(tiles_of(b), 12)

    def edge_masks(b, shifts, strip):
        east, west, north, south = shifts
        top = is_first_row(b.shape, strip)
        end = is_last_row(b.shape, strip)
        bn = jnp.where(end, 0, north(b))
        bs = jnp.where(top, 0, south(b))
        be, bw = east(b), west(b)
        return b, jnp.minimum(b, be), jnp.minimum(b, bn), jnp.minimum(bw, be), jnp.minimum(bs, bn)

    for i, value in enumerate(edge_masks(b, plane_shifts(), False)):
        bmask[i] = value

    for copy in loads[1:5]:
        copy.wait()
    chunk = n_lev // 2
    shape = (chunk, 8, LON)

    def pack_levels(step, carry):
        at = step * chunk
        low = lanes(shape) % 16 < 8
        wl = lanes(shape) % 16

        def field(ref, offset):
            return pack([ref[pl.ds(at, chunk), 8 * g : 8 * g + 8, :] for g in range(8)], offset)

        t, s = field(tr.at[0], 8), field(tr.at[1], 8)
        uu, vv = field(u, 8), field(v, 8)
        kref = kx.at[pl.ds(1, n_lev)]
        kl, kr = field(kref, 4), field(kref, 12)
        eown[pl.ds(at + 2, chunk), 0] = t
        eown[pl.ds(at + 2, chunk), 1] = s
        eown[pl.ds(at + 2, chunk), 2] = uu
        eown[pl.ds(at + 2, chunk), 3] = vv
        kown[pl.ds(at + 1, chunk), 0] = kl
        kown[pl.ds(at + 1, chunk), 1] = kr
        msg_r[pl.ds(at, chunk), 0] = jnp.where(low, t, pltpu.roll(s, 8, 2))
        msg_r[pl.ds(at, chunk), 1] = jnp.where(
            wl == 8, pltpu.roll(kr, LON - 3, 2), jnp.where(low, uu, pltpu.roll(vv, 8, 2))
        )
        msg_l[pl.ds(at, chunk), 0] = jnp.where(low, pltpu.roll(s, LON - 8, 2), t)
        msg_l[pl.ds(at, chunk), 1] = jnp.where(
            wl == 7, pltpu.roll(kl, 3, 2), jnp.where(low, pltpu.roll(vv, LON - 8, 2), uu)
        )
        return carry

    lax.fori_loop(0, n_lev // chunk, pack_levels, 0)
    loads[5].wait()

    @pl.when(has_up & has_dn)
    def _():
        pl.semaphore_wait(barrier, 8)

    @pl.when(jnp.logical_not(has_up & has_dn))
    def _():
        pl.semaphore_wait(barrier, 5)

    top2, end2 = pl.ds(0, 2), pl.ds(n_lev - 2, 2)
    pre2, post2 = pl.ds(0, 2), pl.ds(n_lev + 2, 2)
    lon_r = remote(msg_r, from_l.at[pl.ds(2, n_lev)], LON_R, (right, dep))
    lon_l = remote(msg_l, from_r.at[pl.ds(2, n_lev)], LON_L, (left, dep))
    bot_r = remote(bown.at[0], brecv.at[0], BOT_R, (right, dep))
    bot_l = remote(bown.at[0], brecv.at[1], BOT_L, (left, dep))
    ups = [
        remote(msg_r.at[top2], from_l.at[post2], DG_RU, (right, dep - 1)),
        remote(msg_l.at[top2], from_r.at[post2], DG_LU, (left, dep - 1)),
        remote(eown.at[pl.ds(2, 2)], eown.at[post2], E_U, (lon, dep - 1)),
        remote(kown.at[1], kown.at[n_lev + 1], K_U, (lon, dep - 1)),
        remote(kx.at[1], kx.at[n_lev + 1], KX_U, (lon, dep - 1)),
        remote(kv.at[0], kv.at[n_lev], KV_U, (lon, dep - 1)),
        remote(adv.at[pl.ds(2, 2)], adv.at[post2], ADV_U, (lon, dep - 1)),
    ]
    downs = [
        remote(msg_r.at[end2], from_l.at[pre2], DG_RD, (right, dep + 1)),
        remote(msg_l.at[end2], from_r.at[pre2], DG_LD, (left, dep + 1)),
        remote(eown.at[pl.ds(n_lev, 2)], eown.at[pre2], E_D, (lon, dep + 1)),
        remote(kown.at[n_lev], kown.at[0], K_D, (lon, dep + 1)),
        remote(kx.at[n_lev], kx.at[0], KX_D, (lon, dep + 1)),
        remote(adv.at[pl.ds(n_lev, 2)], adv.at[pre2], ADV_D, (lon, dep + 1)),
    ]
    bot_r.start()
    bot_l.start()

    @pl.when(has_up)
    def _():
        for copy in ups[:-1]:
            copy.start()

    @pl.when(has_dn)
    def _():
        for copy in downs[:-1]:
            copy.start()

    lon_r.start()
    lon_l.start()

    batch = 4

    def transport(at, count):
        def stack(which):
            return jnp.stack([bmask[which] > first + at + i for i in range(count)], axis=0)

        span = pl.ds(at, count)
        c0, c1 = upwind(tr[0, span], tr[1, span], u[span], v[span], stack(1), stack(2), plane_shifts())
        adv[pl.ds(at + 2, count), 0] = c0
        adv[pl.ds(at + 2, count), 1] = c1

    def transport_ends(step, carry):
        transport(step * (n_lev - 2), 2)
        return carry

    def transport_rest(step, carry):
        transport(2 + step * batch, batch)
        return carry

    lax.fori_loop(0, 2, transport_ends, 0)

    @pl.when(has_up)
    def _():
        ups[-1].start()

    @pl.when(has_dn)
    def _():
        downs[-1].start()

    @pl.when(has_dn)
    def _():
        ups[5].wait_recv()

    def e_of(at):
        k = first + at
        k = jnp.where(k < 1, FAR, k)
        return jnp.where(bmask[0] > k, kv[at], 0.0)

    def eliminate(at, carry):
        ratio, prod, spike, p_top, e_here = carry
        e_next = e_of(at + 1)
        recip = 1.0 / (1.0 + e_next + e_here * (1.0 - ratio))
        gain = e_here * recip
        inv[at] = recip
        gdn[at] = gain
        rprod[at] = prod
        ratio = e_next * recip
        rdn[at] = ratio
        spike = spike * gain
        pspk[at] = spike
        p_top = p_top + prod * spike
        return ratio, prod * ratio, spike, p_top, e_next

    zero, one = jnp.zeros(plane, jnp.float32), jnp.ones(plane, jnp.float32)
    _, q_top, p_end, p_top, _ = lax.fori_loop(
        0, n_lev, eliminate, (zero, one, one, zero, e_of(0))
    )
    send_end[0, 0] = p_top
    send_end[0, 1] = p_end
    send_end[1, 0] = q_top
    send_end[1, 1] = rdn[n_lev - 1]
    z_copy = remote(send_end.at[i_end, i_end], zmat, ZM, (lon, in_dev))
    q_copy = remote(qmat, qpart, QM, (lon, 3 - dep))

    @pl.when(outer)
    def _():
        z_copy.start()

    def back_matrix(step, carry):
        p_low, q_low = carry
        at = n_lev - 1 - step
        ratio = rdn[at]
        p = pspk[at] + ratio * p_low
        q = ratio * q_low
        pspk[at] = p
        qspk[at] = q
        return p, q

    lax.fori_loop(0, n_lev, back_matrix, (zero, one))

    lax.fori_loop(0, (n_lev - 4) // batch, transport_rest, 0)

    @pl.when(inner)
    def _():
        z_copy.wait_recv()
        z = zmat[...]
        inv_t = 1.0 / (1.0 - z * send_end[o_end, o_end])
        tmat[0] = inv_t
        beta = z * send_end[i_end, o_end] * inv_t
        tmat[1] = beta
        qmat[...] = send_end[i_end, i_end] + send_end[o_end, i_end] * beta
        q_copy.start()

    def flux_levels(at, count):
        def stack(which, floor, shift):
            parts = []
            for i in range(count):
                k = first + at + i - 1
                parts.append(bmask[which] > jnp.where(k < floor, FAR, k + shift))
            return jnp.stack(parts, axis=0)

        kappa = jnp.where(stack(0, 0, 0), 0.25 * kx[pl.ds(at, count)], 0.0)
        f, w = fluxes(
            [adv[pl.ds(at, count), n] for n in range(2)], [adv[pl.ds(at + 1, count), n] for n in range(2)],
            [adv[pl.ds(at + 2, count), n] for n in range(2)], kappa,
            stack(3, 0, 0), stack(4, 0, 0), stack(0, 1, 1), plane_shifts(),
        )
        for n in range(2):
            flat[pl.ds(at, count), n] = f[n]
            vert[pl.ds(at, count), n] = w[n]

    def flux_rest(step, carry):
        flux_levels(2 + 2 * step, 2)
        return carry

    def flux_ends(step, carry):
        flux_levels(step * n_lev, 2)
        return carry

    lax.fori_loop(0, (n_lev - 2) // 2, flux_rest, 0)

    @pl.when(has_dn)
    def _():
        ups[4].wait_recv()
        ups[6].wait_recv()

    @pl.when(has_up)
    def _():
        downs[4].wait_recv()
        downs[5].wait_recv()

    lax.fori_loop(0, 2, flux_ends, 0)

    chunk = (n_lev + 4) // 2
    shape = (chunk, 8, LON)

    def pack_windows(step, carry):
        at = step * chunk
        low = lanes(shape) % 16 < 8
        for n in range(2):
            parts = [adv[pl.ds(at, chunk), n, 8 * g : 8 * g + 8, :] for g in range(8)]
            gwin[n, pl.ds(at, chunk)] = jnp.where(low, pack(parts, 12), pack(parts, 4))
        return carry

    lax.fori_loop(0, (n_lev + 4) // chunk, pack_windows, 0)

    bot_r.wait_recv()
    bot_l.wait_recv()
    lon_r.wait_recv()
    lon_l.wait_recv()

    @pl.when(has_dn)
    def _():
        for copy in ups[:4]:
            copy.wait_recv()

    @pl.when(has_up)
    def _():
        for copy in downs[:4]:
            copy.wait_recv()

    b_l = jnp.where(lo8, brecv[0], bown[0])
    b_r = jnp.where(lo8, bown[0], brecv[1])
    w_l = jnp.where(lo8, pltpu.roll(b_l, LON - 4, 1), bown[1])
    w_r = jnp.where(lo8, bown[2], pltpu.roll(b_r, 4, 1))
    for side, value in enumerate((b_l, b_r)):
        masks = edge_masks(value, strip_shifts(), True)
        bstrip[0, side] = masks[1]
        bstrip[1, side] = masks[2]
    for side, value in enumerate((w_l, w_r)):
        masks = edge_masks(value, strip_shifts(), True)
        bstrip[2, side] = masks[0]
        bstrip[3, side] = masks[3]
        bstrip[4, side] = masks[4]

    flatshape = (2 * chunk, 8, LON)

    def level_mask(which, start, floor, shift):
        parts = []
        for i in range(chunk):
            k = start + i
            k = jnp.where(k < floor, FAR, k + shift)
            parts.append(bstrip[which] > k)
        return jnp.concatenate(parts, axis=0)

    def join(left_part, right_part):
        return jnp.stack([left_part, right_part], axis=1).reshape(flatshape)

    def strip_transport(step, carry):
        at = step * chunk
        k = first + at - 2
        low = lanes(shape) % 16 < 8
        own = [eown[pl.ds(at, chunk), i] for i in range(4)]
        la, lb = from_l[pl.ds(at, chunk), 0], from_l[pl.ds(at, chunk), 1]
        ra, rb = from_r[pl.ds(at, chunk), 0], from_r[pl.ds(at, chunk), 1]

        def assemble(i, from_left, from_right):
            return join(jnp.where(low, from_left, own[i]), jnp.where(low, own[i], from_right))

        c0 = assemble(0, la, ra)
        c1 = assemble(1, pltpu.roll(la, LON - 8, 2), pltpu.roll(ra, 8, 2))
        uu = assemble(2, lb, rb)
        vv = assemble(3, pltpu.roll(lb, LON - 8, 2), pltpu.roll(rb, 8, 2))
        done = upwind(c0, c1, uu, vv, level_mask(0, k, 0, 0), level_mask(1, k, 0, 0), strip_shifts())
        for n in range(2):
            both = done[n].reshape(chunk, 2, 8, LON)
            g = gwin[n, pl.ds(at, chunk)]
            awin[pl.ds(at, chunk), n, 0] = jnp.where(low, pltpu.roll(both[:, 0], LON - 4, 2), g)
            awin[pl.ds(at, chunk), n, 1] = jnp.where(low, g, pltpu.roll(both[:, 1], 4, 2))
        return carry

    lax.fori_loop(0, (n_lev + 4) // chunk, strip_transport, 0)

    def strip_flux(step, carry):
        at = step * chunk
        k = first + at - 1
        wl = lanes(shape) % 16
        lb, rb = from_l[pl.ds(at + 1, chunk), 1], from_r[pl.ds(at + 1, chunk), 1]
        kl = jnp.where(wl == 3, pltpu.roll(lb, LON - 5, 2), kown[pl.ds(at, chunk), 0])
        kr = jnp.where(wl == 12, pltpu.roll(rb, 5, 2), kown[pl.ds(at, chunk), 1])
        kappa = jnp.where(level_mask(2, k, 0, 0), 0.25 * join(kl, kr), 0.0)

        def window(shift):
            return [awin[pl.ds(at + shift, chunk), n].reshape(flatshape) for n in range(2)]

        f, w = fluxes(
            window(0), window(1), window(2), kappa,
            level_mask(3, k, 0, 0), level_mask(4, k, 0, 0), level_mask(2, k, 1, 1), strip_shifts(),
        )
        for n in range(2):
            sflat[pl.ds(at, chunk), n] = f[n].reshape(chunk, 2, 8, LON)
            svert[pl.ds(at, chunk), n] = w[n].reshape(chunk, 2, 8, LON)
        return carry

    lax.fori_loop(0, (n_lev + 4) // chunk, strip_flux, 0)

    chunk = n_lev
    shape = (chunk, 8, LON)
    flatshape = (2 * chunk, 8, LON)

    def strip_update(step, carry):
        at = step * chunk
        low = lanes(shape) % 16 < 8
        wet = level_mask(2, first + at, 0, 0)
        for n in range(2):
            gain = (
                sflat[pl.ds(at + 1, chunk), n] + svert[pl.ds(at + 2, chunk), n] - svert[pl.ds(at, chunk), n]
            ).reshape(flatshape)
            new = awin[pl.ds(at + 2, chunk), n].reshape(flatshape) + jnp.where(wet, gain, 0.0)
            both = new.reshape(chunk, 2, 8, LON)
            edge[pl.ds(at, chunk), n] = jnp.where(
                low, pltpu.roll(both[:, 1], LON - 4, 2), pltpu.roll(both[:, 0], 4, 2)
            )
        return carry

    lax.fori_loop(0, n_lev // chunk, strip_update, 0)

    yend[...] = jnp.zeros(yend.shape, jnp.float32)
    fval[0] = jnp.zeros((2,) + plane, jnp.float32)
    lane = lanes(plane)
    on_edge = (lane < 6) | (lane >= LON - 6)

    group = 5

    def way_down(step, carry):
        at = step * group
        for n in range(2):
            value, total = fval[at, n], yend[0, n]
            for i in range(group):
                here = at + i
                wet = bmask[0] > first + here
                new = adv[here + 2, n] + jnp.where(
                    wet, flat[here + 1, n] + vert[here + 2, n] - vert[here, n], 0.0
                )
                packed = edge[here, n]
                fixed = jnp.concatenate(
                    [pltpu.roll(packed, (LON - 8 - 16 * g) % LON, 1) for g in range(8)], axis=0
                )
                new = jnp.where(on_edge, fixed, new)
                value = new * inv[here] + gdn[here] * value
                fval[here + 1, n] = value
                total = total + rprod[here] * value
            yend[0, n] = total
        return carry

    lax.fori_loop(0, n_lev // group, way_down, 0)
    yend[1] = fval[n_lev]

    z_val = remote(yend.at[i_end], zval, ZV, (lon, in_dev))
    y_val = remote(yval, ypart, YV, (lon, 3 - dep))
    x_val = remote(xout, xend.at[i_end], XO, (lon, out_dev))

    @pl.when(outer)
    def _():
        z_val.start()
        xend[o_end] = jnp.zeros((2,) + plane, jnp.float32)

    @pl.when(inner)
    def _():
        z_val.wait_recv()
        for n in range(2):
            alpha = (zval[n] + zmat[...] * yend[o_end, n]) * tmat[0]
            xend[o_end, n] = alpha
            yval[n] = yend[i_end, n] + send_end[o_end, i_end] * alpha
        y_val.start()

    def way_up(step, carry):
        at = n_lev - 1 - step
        ratio = rdn[at - 1]
        for n in range(2):
            fval[at, n] = fval[at, n] + ratio * fval[at + 1, n]
        return carry

    lax.fori_loop(0, n_lev - 1, way_up, 0)

    @pl.when(inner)
    def _():
        q_copy.wait_recv()
        y_val.wait_recv()
        q_other = qpart[...]
        inv_m = 1.0 / (1.0 - q_other * qmat[...])
        oo, io = send_end[o_end, o_end], send_end[i_end, o_end]
        for n in range(2):
            x_in = (ypart[n] + q_other * yval[n]) * inv_m
            xout[n] = (yend[o_end, n] + oo * zval[n] + io * x_in) * tmat[0]
            xend[i_end, n] = x_in
        x_val.start()
        for n in range(2):
            xend[o_end, n] = xend[o_end, n] + tmat[1] * xend[i_end, n]

    @pl.when(outer)
    def _():
        x_val.wait_recv()

    part = n_lev // 4
    for i in range(4):
        def finish(at, carry):
            p, q = pspk[at], qspk[at]
            for n in range(2):
                out_hbm[n, at] = fval[at + 1, n] + p * xend[0, n] + q * xend[1, n]
            return carry

        lax.fori_loop(i * part, (i + 1) * part, finish, 0)

    for copy in (lon_r, lon_l, bot_r, bot_l):
        copy.wait_send()

    @pl.when(has_up)
    def _():
        for copy in ups:
            copy.wait_send()

    @pl.when(has_dn)
    def _():
        for copy in downs:
            copy.wait_send()

    @pl.when(outer)
    def _():
        z_copy.wait_send()
        z_val.wait_send()

    @pl.when(inner)
    def _():
        q_copy.wait_send()
        y_val.wait_send()
        x_val.wait_send()


def per_device(n_lon, n_dep, tracers, u_east, v_north, kappa_h, kappa_v, bottom):
    n_lev = tracers.shape[1]
    ext = n_lev + 4

    def f32(*shape):
        return pltpu.VMEM(shape, jnp.float32)

    def i32(*shape):
        return pltpu.VMEM(shape, jnp.int32)

    scratch = [
        f32(2, n_lev, LAT, LON), f32(n_lev, LAT, LON), f32(n_lev, LAT, LON),
        f32(n_lev + 2, LAT, LON), f32(n_lev + 1, LAT, LON), i32(LAT, LON),
        i32(5, LAT, LON), i32(5, 2, 8, LON), i32(3, 8, LON), i32(2, 8, LON),
        f32(ext, 4, 8, LON), f32(ext, 2, 8, LON),
        f32(n_lev, 2, 8, LON), f32(n_lev, 2, 8, LON),
        f32(ext + 1, 2, 8, LON), f32(ext + 1, 2, 8, LON),
        f32(ext, 2, LAT, LON), f32(n_lev + 2, 2, LAT, LON), f32(n_lev + 2, 2, LAT, LON),
        f32(2, ext, 8, LON), f32(ext + 2, 2, 2, 8, LON),
        f32(ext, 2, 2, 8, LON), f32(ext, 2, 2, 8, LON), f32(n_lev, 2, 8, LON),
    ]
    scratch += [f32(n_lev, LAT, LON)] * 6
    scratch += [
        f32(n_lev + 1, 2, LAT, LON), f32(2, 2, LAT, LON), f32(2, 2, LAT, LON),
        f32(LAT, LON), f32(LAT, LON), f32(LAT, LON),
        f32(2, LAT, LON), f32(2, LAT, LON), f32(2, LAT, LON), f32(2, LAT, LON),
        f32(2, 2, LAT, LON), f32(2, LAT, LON),
        pltpu.SemaphoreType.DMA((6,)),
        pltpu.SemaphoreType.DMA((N_COPIES,)), pltpu.SemaphoreType.DMA((N_COPIES,)),
    ]
    hbm = pl.BlockSpec(memory_space=pltpu.HBM)
    return pl.pallas_call(
        functools.partial(kernel, n_lon, n_dep, n_lev),
        out_shape=jax.ShapeDtypeStruct(tracers.shape, jnp.float32),
        in_specs=[hbm] * 6,
        out_specs=pl.BlockSpec(memory_space=pltpu.VMEM),
        scratch_shapes=scratch,
        name="tracer_step",
        compiler_params=pltpu.CompilerParams(
            collective_id=0, has_side_effects=True, vmem_limit_bytes=48 << 20
        ),
    )(*(pltpu.with_memory_space_constraint(a, pltpu.HBM) for a in (tracers, u_east, v_north, kappa_h, kappa_v, bottom)))


def solution(mesh):
    n_lon, n_dep = mesh.shape["lon"], mesh.shape["dep"]
    level = P("dep", None, "lon")
    return jax.shard_map(
        functools.partial(per_device, n_lon, n_dep),
        mesh=mesh,
        in_specs=(P(None, "dep", None, "lon"), level, level, level, level, P(None, "lon")),
        out_specs=P(None, "dep", None, "lon"),
        check_vma=False,
    )
```

```python
import functools

import jax
import jax.numpy as jnp
from jax import lax
from jax.experimental import pallas as pl
from jax.experimental.pallas import tpu as pltpu
from jax.sharding import PartitionSpec as P

MESH = pl.DeviceIdType.MESH
SUB = 4
LAT = 64
LON = 128
THERMAL = 0.2
HALINE = 0.8
FAR = 1 << 20
TB, FB, SC = 4, 2, 12

(LON_R, LON_L, BOT_R, BOT_L, DG_RU, DG_RD, DG_LU, DG_LD, E_U, E_D, K_U, K_D, KX_U, KX_D, KV_U, ADV_U, ADV_D, ZM, QM, ZV, YV, XO) = range(22)
N_COPIES = 22


def lanes(shape):
    return lax.broadcasted_iota(jnp.int32, shape, len(shape) - 1)


def rows(shape):
    return lax.broadcasted_iota(jnp.int32, shape, len(shape) - 2)


def plane_shifts():
    def east(x):
        return pltpu.roll(x, LON - 1, x.ndim - 1)

    def west(x):
        return pltpu.roll(x, 1, x.ndim - 1)

    def north(x):
        return pltpu.roll(x, LAT - 1, x.ndim - 2)

    def south(x):
        return pltpu.roll(x, 1, x.ndim - 2)

    return east, west, north, south


def strip_shifts():
    def east(x):
        return pltpu.roll(x, LON - 1, x.ndim - 1)

    def west(x):
        return pltpu.roll(x, 1, x.ndim - 1)

    def north(x):
        y = pltpu.roll(x, 7, x.ndim - 2)
        return jnp.where(rows(x.shape) == 7, pltpu.roll(y, 112, x.ndim - 1), y)

    def south(x):
        y = pltpu.roll(x, 1, x.ndim - 2)
        return jnp.where(rows(x.shape) == 0, pltpu.roll(y, 16, x.ndim - 1), y)

    return east, west, north, south


def is_first_row(shape, strip):
    if strip:
        return (rows(shape) == 0) & (lanes(shape) < 16)
    return rows(shape) == 0


def is_last_row(shape, strip):
    if strip:
        return (rows(shape) == 7) & (lanes(shape) >= 112)
    return rows(shape) == LAT - 1


def upwind(c0, c1, u, v, face_x, face_y, shifts):
    east, west, north, south = shifts
    u = jnp.where(face_x, u, 0.0)
    v = jnp.where(face_y, v, 0.0)
    up = jnp.maximum(u, 0.0)
    vp = jnp.maximum(v, 0.0)
    ce = up - u
    cn = vp - v
    cw = west(up)
    cs = south(vp)
    keep = 1.0 - up - vp - west(ce) - south(cn)

    def advance(c):
        return keep * c + cw * west(c) + ce * east(c) + cs * south(c) + cn * north(c)

    for _ in range(SUB):
        c0 = advance(c0)
        c1 = advance(c1)
    return c0, c1


def fluxes(low, mid, high, kappa, mask_x, mask_y, mask_z, shifts):
    east, west, north, south = shifts
    gx = [jnp.where(mask_x, east(c) - west(c), 0.0) for c in mid]
    gy = [jnp.where(mask_y, north(c) - south(c), 0.0) for c in mid]
    gz = [jnp.where(mask_z, h - l, 0.0) for l, h in zip(low, high)]

    rx, ry, rz = (g[1] - (THERMAL / HALINE) * g[0] for g in (gx, gy, gz))
    ratio = rz / ((4.0 / HALINE**2) + rx * rx + ry * ry + rz * rz)
    sx, sy = rx * ratio, ry * ratio
    flat, vert = [], []
    for n in range(2):
        fx = kappa * (gx[n] + sx * gz[n])
        fy = kappa * (gy[n] + sy * gz[n])
        vert.append(sx * fx + sy * fy)
        flat.append((east(fx) - west(fx)) + (north(fy) - south(fy)))
    return flat, vert


def pack(tiles, offset):
    group = lanes(tiles[0].shape) // 16
    out = None
    for g in range(8):
        moved = pltpu.roll(tiles[g], (16 * g + offset) % LON, tiles[g].ndim - 1)
        out = moved if out is None else jnp.where(group == g, moved, out)
    return out


def tiles_of(plane):
    return [plane[..., 8 * g : 8 * g + 8, :] for g in range(8)]


def kernel(
    n_lon, n_dep, n_lev,
    tr_hbm, u_hbm, v_hbm, kh_hbm, kv_hbm, bot_hbm,
    out_hbm,
    tr, u, v, kx, kv, bot,
    bmask, bstrip, bown, brecv,
    eown, kown, msg_r, msg_l, from_l, from_r,
    adv, flat, vert, gwin, awin, sflat, svert, edge,
    inv, gdn, rdn, rprod, pspk, qspk, fval, yend, send_end,
    zmat, qmat, qpart, zval, yval, ypart, xout, xend, tmat,
    in_sem, ssem, rsem,
):
    lon = lax.axis_index("lon")
    dep = lax.axis_index("dep")
    right = lax.rem(lon + 1, n_lon)
    left = lax.rem(lon + n_lon - 1, n_lon)
    first = dep * n_lev
    has_up = dep > 0
    has_dn = dep < n_dep - 1
    inner = (dep == 1) | (dep == 2)
    outer = jnp.logical_not(inner)
    o_end = jnp.where(dep < 2, 0, 1)
    i_end = 1 - o_end
    out_dev = jnp.where(dep < 2, 0, 3)
    in_dev = jnp.where(dep < 2, 1, 2)
    plane = (LAT, LON)
    tile = (8, LON)

    def remote(src, dst, index, device):
        return pltpu.make_async_remote_copy(
            src_ref=src, dst_ref=dst, send_sem=ssem.at[index], recv_sem=rsem.at[index],
            device_id=device, device_id_type=MESH,
        )

    loads = [
        pltpu.make_async_copy(bot_hbm, bot, in_sem.at[0]),
        pltpu.make_async_copy(tr_hbm, tr, in_sem.at[1]),
        pltpu.make_async_copy(u_hbm, u, in_sem.at[2]),
        pltpu.make_async_copy(v_hbm, v, in_sem.at[3]),
        pltpu.make_async_copy(kh_hbm, kx.at[pl.ds(1, n_lev)], in_sem.at[4]),
        pltpu.make_async_copy(kv_hbm, kv.at[pl.ds(0, n_lev)], in_sem.at[5]),
    ]
    for copy in loads:
        copy.start()

    barrier = pltpu.get_barrier_semaphore()

    def greet(device):
        pl.semaphore_signal(barrier, inc=1, device_id=device, device_id_type=MESH)

    greet((right, dep))
    greet((left, dep))

    @pl.when(has_up)
    def _():
        greet((lon, dep - 1))
        greet((right, dep - 1))
        greet((left, dep - 1))

    @pl.when(has_dn)
    def _():
        greet((lon, dep + 1))
        greet((right, dep + 1))
        greet((left, dep + 1))

    def clear(ref, start, count):
        part = ref.at[pl.ds(start, count)]
        part[...] = jnp.zeros(part.shape, part.dtype)

    @pl.when(jnp.logical_not(has_up))
    def _():
        clear(from_l, 0, 2)
        clear(from_r, 0, 2)
        clear(eown, 0, 2)
        clear(kown, 0, 1)
        clear(kx, 0, 1)
        clear(adv, 0, 2)

    @pl.when(jnp.logical_not(has_dn))
    def _():
        clear(from_l, n_lev + 2, 2)
        clear(from_r, n_lev + 2, 2)
        clear(eown, n_lev + 2, 2)
        clear(kown, n_lev + 1, 1)
        clear(kx, n_lev + 1, 1)
        clear(adv, n_lev + 2, 2)
        clear(kv, n_lev, 1)

    clear(kown, n_lev + 2, 2)
    clear(awin, n_lev + 4, 2)

    lo8 = lanes(tile) % 16 < 8

    loads[0].wait()
    b = bot[...]
    bown[0] = pack(tiles_of(b), 8)
    bown[1] = pack(tiles_of(b), 4)
    bown[2] = pack(tiles_of(b), 12)

    def edge_masks(b, shifts, strip):
        east, west, north, south = shifts
        top = is_first_row(b.shape, strip)
        end = is_last_row(b.shape, strip)
        bn = jnp.where(end, 0, north(b))
        bs = jnp.where(top, 0, south(b))
        be, bw = east(b), west(b)
        return b, jnp.minimum(b, be), jnp.minimum(b, bn), jnp.minimum(bw, be), jnp.minimum(bs, bn)

    for i, value in enumerate(edge_masks(b, plane_shifts(), False)):
        bmask[i] = value

    for copy in loads[1:5]:
        copy.wait()
    chunk = n_lev // 2
    shape = (chunk, 8, LON)

    def pack_levels(step, carry):
        at = step * chunk
        low = lanes(shape) % 16 < 8
        wl = lanes(shape) % 16

        def field(ref, offset):
            return pack([ref[pl.ds(at, chunk), 8 * g : 8 * g + 8, :] for g in range(8)], offset)

        t, s = field(tr.at[0], 8), field(tr.at[1], 8)
        uu, vv = field(u, 8), field(v, 8)
        kref = kx.at[pl.ds(1, n_lev)]
        kl, kr = field(kref, 4), field(kref, 12)
        eown[pl.ds(at + 2, chunk), 0] = t
        eown[pl.ds(at + 2, chunk), 1] = s
        eown[pl.ds(at + 2, chunk), 2] = uu
        eown[pl.ds(at + 2, chunk), 3] = vv
        kown[pl.ds(at + 1, chunk), 0] = kl
        kown[pl.ds(at + 1, chunk), 1] = kr
        msg_r[pl.ds(at, chunk), 0] = jnp.where(low, t, pltpu.roll(s, 8, 2))
        msg_r[pl.ds(at, chunk), 1] = jnp.where(
            wl == 10, pltpu.roll(kr, LON - 1, 2), jnp.where(low, uu, pltpu.roll(vv, 8, 2))
        )
        msg_l[pl.ds(at, chunk), 0] = jnp.where(low, pltpu.roll(s, LON - 8, 2), t)
        msg_l[pl.ds(at, chunk), 1] = jnp.where(
            wl == 5, pltpu.roll(kl, 1, 2), jnp.where(low, pltpu.roll(vv, LON - 8, 2), uu)
        )
        return carry

    lax.fori_loop(0, n_lev // chunk, pack_levels, 0)

    guests = n_lev // 4
    hosts = n_lev - guests
    slot = lanes((guests, 8, LON)) % 8
    for i in range(2):
        guest_r, guest_l = msg_r[pl.ds(hosts, guests), i], msg_l[pl.ds(hosts, guests), i]
        for j in range(3):
            span = pl.ds(j * guests, guests)
            msg_r[span, i] = jnp.where(slot < 2, pltpu.roll(guest_r, LON - 2 - 2 * j, 2), msg_r[span, i])
            msg_l[span, i] = jnp.where(slot >= 6, pltpu.roll(guest_l, 6 - 2 * j, 2), msg_l[span, i])
    loads[5].wait()

    @pl.when(has_up & has_dn)
    def _():
        pl.semaphore_wait(barrier, 8)

    @pl.when(jnp.logical_not(has_up & has_dn))
    def _():
        pl.semaphore_wait(barrier, 5)

    top2, end2 = pl.ds(0, 2), pl.ds(n_lev - 2, 2)
    pre2, post2 = pl.ds(0, 2), pl.ds(n_lev + 2, 2)
    lon_r = remote(msg_r.at[pl.ds(0, hosts)], from_l.at[pl.ds(2, hosts)], LON_R, (right, dep))
    lon_l = remote(msg_l.at[pl.ds(0, hosts)], from_r.at[pl.ds(2, hosts)], LON_L, (left, dep))
    bot_r = remote(bown.at[0], brecv.at[0], BOT_R, (right, dep))
    bot_l = remote(bown.at[0], brecv.at[1], BOT_L, (left, dep))
    ups = [
        remote(msg_r.at[top2], from_l.at[post2], DG_RU, (right, dep - 1)),
        remote(msg_l.at[top2], from_r.at[post2], DG_LU, (left, dep - 1)),
        remote(eown.at[pl.ds(2, 2)], eown.at[post2], E_U, (lon, dep - 1)),
        remote(kown.at[1], kown.at[n_lev + 1], K_U, (lon, dep - 1)),
        remote(kx.at[1], kx.at[n_lev + 1], KX_U, (lon, dep - 1)),
        remote(kv.at[0], kv.at[n_lev], KV_U, (lon, dep - 1)),
        remote(adv.at[pl.ds(2, 2)], adv.at[post2], ADV_U, (lon, dep - 1)),
    ]
    downs = [
        remote(msg_r.at[end2], from_l.at[pre2], DG_RD, (right, dep + 1)),
        remote(msg_l.at[end2], from_r.at[pre2], DG_LD, (left, dep + 1)),
        remote(eown.at[pl.ds(n_lev, 2)], eown.at[pre2], E_D, (lon, dep + 1)),
        remote(kown.at[n_lev], kown.at[0], K_D, (lon, dep + 1)),
        remote(kx.at[n_lev], kx.at[0], KX_D, (lon, dep + 1)),
        remote(adv.at[pl.ds(n_lev, 2)], adv.at[pre2], ADV_D, (lon, dep + 1)),
    ]
    bot_r.start()
    bot_l.start()

    @pl.when(has_up)
    def _():
        for copy in ups[:-1]:
            copy.start()

    @pl.when(has_dn)
    def _():
        for copy in downs[:-1]:
            copy.start()

    lon_r.start()
    lon_l.start()

    batch = TB

    def transport(at, count):
        def stack(which):
            return jnp.stack([bmask[which] > first + at + i for i in range(count)], axis=0)

        span = pl.ds(at, count)
        c0, c1 = upwind(tr[0, span], tr[1, span], u[span], v[span], stack(1), stack(2), plane_shifts())
        adv[pl.ds(at + 2, count), 0] = c0
        adv[pl.ds(at + 2, count), 1] = c1

    def transport_ends(step, carry):
        transport(step * (n_lev - 2), 2)
        return carry

    def transport_rest(step, carry):
        transport(2 + step * batch, batch)
        return carry

    lax.fori_loop(0, 2, transport_ends, 0)

    @pl.when(has_up)
    def _():
        ups[-1].start()

    @pl.when(has_dn)
    def _():
        downs[-1].start()

    lax.fori_loop(0, (n_lev - 4) // batch, transport_rest, 0)

    def flux_levels(at, count):
        def stack(which, floor, shift):
            parts = []
            for i in range(count):
                k = first + at + i - 1
                parts.append(bmask[which] > jnp.where(k < floor, FAR, k + shift))
            return jnp.stack(parts, axis=0)

        kappa = jnp.where(stack(0, 0, 0), 0.25 * kx[pl.ds(at, count)], 0.0)
        f, w = fluxes(
            [adv[pl.ds(at, count), n] for n in range(2)], [adv[pl.ds(at + 1, count), n] for n in range(2)],
            [adv[pl.ds(at + 2, count), n] for n in range(2)], kappa,
            stack(3, 0, 0), stack(4, 0, 0), stack(0, 1, 1), plane_shifts(),
        )
        for n in range(2):
            flat[pl.ds(at, count), n] = f[n]
            vert[pl.ds(at, count), n] = w[n]

    def flux_rest(step, carry):
        flux_levels(2 + FB * step, FB)
        return carry

    def flux_ends(step, carry):
        flux_levels(step * n_lev, 2)
        return carry

    lax.fori_loop(0, (n_lev - 2) // FB, flux_rest, 0)

    @pl.when(has_dn)
    def _():
        ups[5].wait_recv()

    def e_of(at):
        k = first + at
        k = jnp.where(k < 1, FAR, k)
        return jnp.where(bmask[0] > k, kv[at], 0.0)

    def eliminate(at, carry):
        ratio, prod, spike, p_top, e_here = carry
        e_next = e_of(at + 1)
        recip = 1.0 / (1.0 + e_next + e_here * (1.0 - ratio))
        gain = e_here * recip
        inv[at] = recip
        gdn[at] = gain
        rprod[at] = prod
        ratio = e_next * recip
        rdn[at] = ratio
        spike = spike * gain
        pspk[at] = spike
        p_top = p_top + prod * spike
        return ratio, prod * ratio, spike, p_top, e_next

    zero, one = jnp.zeros(plane, jnp.float32), jnp.ones(plane, jnp.float32)
    _, q_top, p_end, p_top, _ = lax.fori_loop(
        0, n_lev, eliminate, (zero, one, one, zero, e_of(0))
    )
    send_end[0, 0] = p_top
    send_end[0, 1] = p_end
    send_end[1, 0] = q_top
    send_end[1, 1] = rdn[n_lev - 1]
    z_copy = remote(send_end.at[i_end, i_end], zmat, ZM, (lon, in_dev))
    q_copy = remote(qmat, qpart, QM, (lon, 3 - dep))

    @pl.when(outer)
    def _():
        z_copy.start()

    def back_matrix(step, carry):
        p_low, q_low = carry
        at = n_lev - 1 - step
        ratio = rdn[at]
        p = pspk[at] + ratio * p_low
        q = ratio * q_low
        pspk[at] = p
        qspk[at] = q
        return p, q

    lax.fori_loop(0, n_lev, back_matrix, (zero, one))

    @pl.when(has_dn)
    def _():
        ups[4].wait_recv()
        ups[6].wait_recv()

    @pl.when(has_up)
    def _():
        downs[4].wait_recv()
        downs[5].wait_recv()

    lax.fori_loop(0, 2, flux_ends, 0)

    @pl.when(inner)
    def _():
        z_copy.wait_recv()
        z = zmat[...]
        inv_t = 1.0 / (1.0 - z * send_end[o_end, o_end])
        tmat[0] = inv_t
        beta = z * send_end[i_end, o_end] * inv_t
        tmat[1] = beta
        qmat[...] = send_end[i_end, i_end] + send_end[o_end, i_end] * beta
        q_copy.start()

    chunk = SC
    shape = (chunk, 8, LON)

    def pack_windows(step, carry):
        at = step * chunk
        low = lanes(shape) % 16 < 8
        for n in range(2):
            parts = [adv[pl.ds(at, chunk), n, 8 * g : 8 * g + 8, :] for g in range(8)]
            gwin[n, pl.ds(at, chunk)] = jnp.where(low, pack(parts, 12), pack(parts, 4))
        return carry

    lax.fori_loop(0, (n_lev + 4) // chunk, pack_windows, 0)

    bot_r.wait_recv()
    bot_l.wait_recv()
    lon_r.wait_recv()
    lon_l.wait_recv()
    for i in range(2):
        guest_l = guest_r = None
        for j in range(3):
            span = pl.ds(2 + j * guests, guests)
            part_l = pltpu.roll(from_l[span, i], 2 + 2 * j, 2)
            part_r = pltpu.roll(from_r[span, i], LON - 6 + 2 * j, 2)
            guest_l = part_l if j == 0 else jnp.where(slot >= 2 + 2 * j, part_l, guest_l)
            guest_r = part_r if j == 0 else jnp.where(slot >= 2 * j, part_r, guest_r)
        from_l[pl.ds(2 + hosts, guests), i] = guest_l
        from_r[pl.ds(2 + hosts, guests), i] = guest_r

    @pl.when(has_dn)
    def _():
        for copy in ups[:4]:
            copy.wait_recv()

    @pl.when(has_up)
    def _():
        for copy in downs[:4]:
            copy.wait_recv()

    b_l = jnp.where(lo8, brecv[0], bown[0])
    b_r = jnp.where(lo8, bown[0], brecv[1])
    w_l = jnp.where(lo8, pltpu.roll(b_l, LON - 4, 1), bown[1])
    w_r = jnp.where(lo8, bown[2], pltpu.roll(b_r, 4, 1))
    for side, value in enumerate((b_l, b_r)):
        masks = edge_masks(value, strip_shifts(), True)
        bstrip[0, side] = masks[1]
        bstrip[1, side] = masks[2]
    for side, value in enumerate((w_l, w_r)):
        masks = edge_masks(value, strip_shifts(), True)
        bstrip[2, side] = masks[0]
        bstrip[3, side] = masks[3]
        bstrip[4, side] = masks[4]

    flatshape = (2 * chunk, 8, LON)

    def level_mask(which, start, floor, shift):
        parts = []
        for i in range(chunk):
            k = start + i
            k = jnp.where(k < floor, FAR, k + shift)
            parts.append(bstrip[which] > k)
        return jnp.concatenate(parts, axis=0)

    def join(left_part, right_part):
        return jnp.stack([left_part, right_part], axis=1).reshape(flatshape)

    def strip_transport(step, carry):
        at = step * chunk
        k = first + at - 2
        low = lanes(shape) % 16 < 8
        own = [eown[pl.ds(at, chunk), i] for i in range(4)]
        la, lb = from_l[pl.ds(at, chunk), 0], from_l[pl.ds(at, chunk), 1]
        ra, rb = from_r[pl.ds(at, chunk), 0], from_r[pl.ds(at, chunk), 1]

        def assemble(i, from_left, from_right):
            return join(jnp.where(low, from_left, own[i]), jnp.where(low, own[i], from_right))

        c0 = assemble(0, la, ra)
        c1 = assemble(1, pltpu.roll(la, LON - 8, 2), pltpu.roll(ra, 8, 2))
        uu = assemble(2, lb, rb)
        vv = assemble(3, pltpu.roll(lb, LON - 8, 2), pltpu.roll(rb, 8, 2))
        done = upwind(c0, c1, uu, vv, level_mask(0, k, 0, 0), level_mask(1, k, 0, 0), strip_shifts())
        for n in range(2):
            both = done[n].reshape(chunk, 2, 8, LON)
            g = gwin[n, pl.ds(at, chunk)]
            awin[pl.ds(at, chunk), n, 0] = jnp.where(low, pltpu.roll(both[:, 0], LON - 4, 2), g)
            awin[pl.ds(at, chunk), n, 1] = jnp.where(low, g, pltpu.roll(both[:, 1], 4, 2))
        return carry

    lax.fori_loop(0, (n_lev + 4) // chunk, strip_transport, 0)

    def strip_flux(step, carry):
        at = step * chunk
        k = first + at - 1
        wl = lanes(shape) % 16
        lb, rb = from_l[pl.ds(at + 1, chunk), 1], from_r[pl.ds(at + 1, chunk), 1]
        kl = jnp.where(wl == 3, pltpu.roll(lb, LON - 7, 2), kown[pl.ds(at, chunk), 0])
        kr = jnp.where(wl == 12, pltpu.roll(rb, 7, 2), kown[pl.ds(at, chunk), 1])
        kappa = jnp.where(level_mask(2, k, 0, 0), 0.25 * join(kl, kr), 0.0)

        def window(shift):
            return [awin[pl.ds(at + shift, chunk), n].reshape(flatshape) for n in range(2)]

        f, w = fluxes(
            window(0), window(1), window(2), kappa,
            level_mask(3, k, 0, 0), level_mask(4, k, 0, 0), level_mask(2, k, 1, 1), strip_shifts(),
        )
        for n in range(2):
            sflat[pl.ds(at, chunk), n] = f[n].reshape(chunk, 2, 8, LON)
            svert[pl.ds(at, chunk), n] = w[n].reshape(chunk, 2, 8, LON)
        return carry

    lax.fori_loop(0, (n_lev + 4) // chunk, strip_flux, 0)

    chunk = n_lev
    shape = (chunk, 8, LON)
    flatshape = (2 * chunk, 8, LON)

    def strip_update(step, carry):
        at = step * chunk
        low = lanes(shape) % 16 < 8
        wet = level_mask(2, first + at, 0, 0)
        for n in range(2):
            gain = (
                sflat[pl.ds(at + 1, chunk), n] + svert[pl.ds(at + 2, chunk), n] - svert[pl.ds(at, chunk), n]
            ).reshape(flatshape)
            new = awin[pl.ds(at + 2, chunk), n].reshape(flatshape) + jnp.where(wet, gain, 0.0)
            both = new.reshape(chunk, 2, 8, LON)
            edge[pl.ds(at, chunk), n] = jnp.where(
                low, pltpu.roll(both[:, 1], LON - 4, 2), pltpu.roll(both[:, 0], 4, 2)
            )
        return carry

    lax.fori_loop(0, n_lev // chunk, strip_update, 0)

    yend[...] = jnp.zeros(yend.shape, jnp.float32)
    fval[0] = jnp.zeros((2,) + plane, jnp.float32)
    lane = lanes(plane)
    on_edge = (lane < 6) | (lane >= LON - 6)

    group = 5

    def way_down(step, carry):
        at = step * group
        for n in range(2):
            value, total = fval[at, n], yend[0, n]
            for i in range(group):
                here = at + i
                wet = bmask[0] > first + here
                new = adv[here + 2, n] + jnp.where(
                    wet, flat[here + 1, n] + vert[here + 2, n] - vert[here, n], 0.0
                )
                packed = edge[here, n]
                fixed = jnp.concatenate(
                    [pltpu.roll(packed, (LON - 8 - 16 * g) % LON, 1) for g in range(8)], axis=0
                )
                new = jnp.where(on_edge, fixed, new)
                value = new * inv[here] + gdn[here] * value
                fval[here + 1, n] = value
                total = total + rprod[here] * value
            yend[0, n] = total
        return carry

    lax.fori_loop(0, n_lev // group, way_down, 0)
    yend[1] = fval[n_lev]

    z_val = remote(yend.at[i_end], zval, ZV, (lon, in_dev))
    y_val = remote(yval, ypart, YV, (lon, 3 - dep))
    x_val = remote(xout, xend.at[i_end], XO, (lon, out_dev))

    @pl.when(outer)
    def _():
        z_val.start()
        xend[o_end] = jnp.zeros((2,) + plane, jnp.float32)

    @pl.when(inner)
    def _():
        z_val.wait_recv()
        for n in range(2):
            alpha = (zval[n] + zmat[...] * yend[o_end, n]) * tmat[0]
            xend[o_end, n] = alpha
            yval[n] = yend[i_end, n] + send_end[o_end, i_end] * alpha
        y_val.start()

    def way_up(step, carry):
        at = n_lev - 1 - step
        ratio = rdn[at - 1]
        for n in range(2):
            fval[at, n] = fval[at, n] + ratio * fval[at + 1, n]
        return carry

    lax.fori_loop(0, n_lev - 1, way_up, 0)

    @pl.when(inner)
    def _():
        q_copy.wait_recv()
        y_val.wait_recv()
        q_other = qpart[...]
        inv_m = 1.0 / (1.0 - q_other * qmat[...])
        oo, io = send_end[o_end, o_end], send_end[i_end, o_end]
        for n in range(2):
            x_in = (ypart[n] + q_other * yval[n]) * inv_m
            xout[n] = (yend[o_end, n] + oo * zval[n] + io * x_in) * tmat[0]
            xend[i_end, n] = x_in
        x_val.start()
        for n in range(2):
            xend[o_end, n] = xend[o_end, n] + tmat[1] * xend[i_end, n]

    @pl.when(outer)
    def _():
        x_val.wait_recv()

    part = n_lev // 4
    for i in range(4):
        def finish(at, carry):
            p, q = pspk[at], qspk[at]
            for n in range(2):
                out_hbm[n, at] = fval[at + 1, n] + p * xend[0, n] + q * xend[1, n]
            return carry

        lax.fori_loop(i * part, (i + 1) * part, finish, 0)

    for copy in (lon_r, lon_l, bot_r, bot_l):
        copy.wait_send()

    @pl.when(has_up)
    def _():
        for copy in ups:
            copy.wait_send()

    @pl.when(has_dn)
    def _():
        for copy in downs:
            copy.wait_send()

    @pl.when(outer)
    def _():
        z_copy.wait_send()
        z_val.wait_send()

    @pl.when(inner)
    def _():
        q_copy.wait_send()
        y_val.wait_send()
        x_val.wait_send()


def per_device(n_lon, n_dep, tracers, u_east, v_north, kappa_h, kappa_v, bottom):
    n_lev = tracers.shape[1]
    ext = n_lev + 4

    def f32(*shape):
        return pltpu.VMEM(shape, jnp.float32)

    def i32(*shape):
        return pltpu.VMEM(shape, jnp.int32)

    scratch = [
        f32(2, n_lev, LAT, LON), f32(n_lev, LAT, LON), f32(n_lev, LAT, LON),
        f32(n_lev + 2, LAT, LON), f32(n_lev + 1, LAT, LON), i32(LAT, LON),
        i32(5, LAT, LON), i32(5, 2, 8, LON), i32(3, 8, LON), i32(2, 8, LON),
        f32(ext, 4, 8, LON), f32(ext, 2, 8, LON),
        f32(n_lev, 2, 8, LON), f32(n_lev, 2, 8, LON),
        f32(ext + 1, 2, 8, LON), f32(ext + 1, 2, 8, LON),
        f32(ext, 2, LAT, LON), f32(n_lev + 2, 2, LAT, LON), f32(n_lev + 2, 2, LAT, LON),
        f32(2, ext, 8, LON), f32(ext + 2, 2, 2, 8, LON),
        f32(ext, 2, 2, 8, LON), f32(ext, 2, 2, 8, LON), f32(n_lev, 2, 8, LON),
    ]
    scratch += [f32(n_lev, LAT, LON)] * 6
    scratch += [
        f32(n_lev + 1, 2, LAT, LON), f32(2, 2, LAT, LON), f32(2, 2, LAT, LON),
        f32(LAT, LON), f32(LAT, LON), f32(LAT, LON),
        f32(2, LAT, LON), f32(2, LAT, LON), f32(2, LAT, LON), f32(2, LAT, LON),
        f32(2, 2, LAT, LON), f32(2, LAT, LON),
        pltpu.SemaphoreType.DMA((6,)),
        pltpu.SemaphoreType.DMA((N_COPIES,)), pltpu.SemaphoreType.DMA((N_COPIES,)),
    ]
    hbm = pl.BlockSpec(memory_space=pltpu.HBM)
    return pl.pallas_call(
        functools.partial(kernel, n_lon, n_dep, n_lev),
        out_shape=jax.ShapeDtypeStruct(tracers.shape, jnp.float32),
        in_specs=[hbm] * 6,
        out_specs=pl.BlockSpec(memory_space=pltpu.VMEM),
        scratch_shapes=scratch,
        name="tracer_step",
        compiler_params=pltpu.CompilerParams(
            collective_id=0, has_side_effects=True, vmem_limit_bytes=48 << 20
        ),
    )(*(pltpu.with_memory_space_constraint(a, pltpu.HBM) for a in (tracers, u_east, v_north, kappa_h, kappa_v, bottom)))


def solution(mesh):
    n_lon, n_dep = mesh.shape["lon"], mesh.shape["dep"]
    level = P("dep", None, "lon")
    return jax.shard_map(
        functools.partial(per_device, n_lon, n_dep),
        mesh=mesh,
        in_specs=(P(None, "dep", None, "lon"), level, level, level, level, P(None, "lon")),
        out_specs=P(None, "dep", None, "lon"),
        check_vma=False,
    )
```

```python
import functools

import jax
import jax.numpy as jnp
from jax import lax
from jax.experimental import pallas as pl
from jax.experimental.pallas import tpu as pltpu
from jax.sharding import PartitionSpec as P

MESH = pl.DeviceIdType.MESH
SUB = 4
LAT = 64
LON = 128
THERMAL = 0.2
HALINE = 0.8
FAR = 1 << 20
TB, FB, FC, NQ = 8, 2, 12, 2

(LON_R, LON_L, BOT_R, BOT_L, DG_RU, DG_RD, DG_LU, DG_LD, E_U, E_D, K_U, K_D, KX_U, KX_D, KV_U, ADV_U, ADV_D, ZM, QM) = range(19)
ZV, YV, XO, LON2 = 19, 21, 23, 25
N_COPIES = 27


def lanes(shape):
    return lax.broadcasted_iota(jnp.int32, shape, len(shape) - 1)


def rows(shape):
    return lax.broadcasted_iota(jnp.int32, shape, len(shape) - 2)


def plane_shifts():
    def east(x):
        return pltpu.roll(x, LON - 1, x.ndim - 1)

    def west(x):
        return pltpu.roll(x, 1, x.ndim - 1)

    def north(x):
        return pltpu.roll(x, LAT - 1, x.ndim - 2)

    def south(x):
        return pltpu.roll(x, 1, x.ndim - 2)

    return east, west, north, south


def strip_shifts():
    def east(x):
        return pltpu.roll(x, LON - 1, x.ndim - 1)

    def west(x):
        return pltpu.roll(x, 1, x.ndim - 1)

    def north(x):
        y = pltpu.roll(x, 7, x.ndim - 2)
        return jnp.where(rows(x.shape) == 7, pltpu.roll(y, 112, x.ndim - 1), y)

    def south(x):
        y = pltpu.roll(x, 1, x.ndim - 2)
        return jnp.where(rows(x.shape) == 0, pltpu.roll(y, 16, x.ndim - 1), y)

    return east, west, north, south


def is_first_row(shape, strip):
    if strip:
        return (rows(shape) == 0) & (lanes(shape) < 16)
    return rows(shape) == 0


def is_last_row(shape, strip):
    if strip:
        return (rows(shape) == 7) & (lanes(shape) >= 112)
    return rows(shape) == LAT - 1


def upwind(c0, c1, u, v, face_x, face_y, shifts):
    east, west, north, south = shifts
    u = jnp.where(face_x, u, 0.0)
    v = jnp.where(face_y, v, 0.0)
    up = jnp.maximum(u, 0.0)
    vp = jnp.maximum(v, 0.0)
    ce = up - u
    cn = vp - v
    cw = west(up)
    cs = south(vp)
    keep = 1.0 - up - vp - west(ce) - south(cn)

    def advance(c):
        return keep * c + cw * west(c) + ce * east(c) + cs * south(c) + cn * north(c)

    for _ in range(SUB):
        c0 = advance(c0)
        c1 = advance(c1)
    return c0, c1


def fluxes(low, mid, high, north, south, kappa, mask_x, mask_y, mask_z):
    def east(x):
        return pltpu.roll(x, LON - 1, x.ndim - 1)

    def west(x):
        return pltpu.roll(x, 1, x.ndim - 1)

    gx = [jnp.where(mask_x, east(c) - west(c), 0.0) for c in mid]
    gy = [jnp.where(mask_y, a - b, 0.0) for a, b in zip(north, south)]
    gz = [jnp.where(mask_z, a - b, 0.0) for a, b in zip(high, low)]
    rx, ry, rz = (g[1] - (THERMAL / HALINE) * g[0] for g in (gx, gy, gz))
    ratio = rz / ((4.0 / HALINE**2) + rx * rx + ry * ry + rz * rz)
    sx, sy = rx * ratio, ry * ratio
    flat, side, vert = [], [], []
    for n in range(2):
        fx = kappa * (gx[n] + sx * gz[n])
        fy = kappa * (gy[n] + sy * gz[n])
        vert.append(sx * fx + sy * fy)
        flat.append(east(fx) - west(fx))
        side.append(fy)
    return flat, side, vert


def pack(tiles, offset):
    group = lanes(tiles[0].shape) // 16
    out = None
    for g in range(8):
        moved = pltpu.roll(tiles[g], (16 * g + offset) % LON, tiles[g].ndim - 1)
        out = moved if out is None else jnp.where(group == g, moved, out)
    return out


def tiles_of(plane):
    return [plane[..., 8 * g : 8 * g + 8, :] for g in range(8)]


def kernel(
    n_lon, n_dep, n_lev,
    tr_hbm, u_hbm, v_hbm, kh_hbm, kv_hbm, bot_hbm,
    out_hbm,
    tr, u, v, kx, kv, bot,
    bmask, bstrip, bown, brecv,
    eown, kown, msg_r, msg_l, from_l, from_r,
    adv, flat, vert, gwin, awin, sflat, svert, edge,
    inv, gdn, rdn, rprod, pspk, qspk, fval, yend, send_end,
    zmat, qmat, qpart, zval, yval, ypart, xout, xend, tmat,
    in_sem, ssem, rsem,
):
    lon = lax.axis_index("lon")
    dep = lax.axis_index("dep")
    right = lax.rem(lon + 1, n_lon)
    left = lax.rem(lon + n_lon - 1, n_lon)
    first = dep * n_lev
    has_up = dep > 0
    has_dn = dep < n_dep - 1
    inner = (dep == 1) | (dep == 2)
    outer = jnp.logical_not(inner)
    o_end = jnp.where(dep < 2, 0, 1)
    i_end = 1 - o_end
    out_dev = jnp.where(dep < 2, 0, 3)
    in_dev = jnp.where(dep < 2, 1, 2)
    plane = (LAT, LON)
    tile = (8, LON)

    def remote(src, dst, index, device):
        return pltpu.make_async_remote_copy(
            src_ref=src, dst_ref=dst, send_sem=ssem.at[index], recv_sem=rsem.at[index],
            device_id=device, device_id_type=MESH,
        )

    part = n_lev // NQ
    load_bot = pltpu.make_async_copy(bot_hbm, bot, in_sem.at[0])
    load_kv = pltpu.make_async_copy(kv_hbm, kv.at[pl.ds(0, n_lev)], in_sem.at[1])
    load_bot.start()
    loads = []
    for i in range(NQ):
        span = pl.ds(i * part, part)
        loads.append([
            pltpu.make_async_copy(tr_hbm.at[:, span], tr.at[:, span], in_sem.at[4 * i + 2]),
            pltpu.make_async_copy(u_hbm.at[span], u.at[span], in_sem.at[4 * i + 3]),
            pltpu.make_async_copy(v_hbm.at[span], v.at[span], in_sem.at[4 * i + 4]),
            pltpu.make_async_copy(kh_hbm.at[span], kx.at[pl.ds(1 + i * part, part)], in_sem.at[4 * i + 5]),
        ])
        for copy in loads[-1]:
            copy.start()
    load_kv.start()

    barrier = pltpu.get_barrier_semaphore()

    def greet(device):
        pl.semaphore_signal(barrier, inc=1, device_id=device, device_id_type=MESH)

    greet((right, dep))
    greet((left, dep))

    @pl.when(has_up)
    def _():
        greet((lon, dep - 1))
        greet((right, dep - 1))
        greet((left, dep - 1))

    @pl.when(has_dn)
    def _():
        greet((lon, dep + 1))
        greet((right, dep + 1))
        greet((left, dep + 1))

    def clear(ref, start, count):
        part = ref.at[pl.ds(start, count)]
        part[...] = jnp.zeros(part.shape, part.dtype)

    @pl.when(jnp.logical_not(has_up))
    def _():
        clear(from_l, 0, 2)
        clear(from_r, 0, 2)
        clear(eown, 0, 2)
        clear(kown, 0, 1)
        clear(kx, 0, 1)
        clear(adv, 0, 2)

    @pl.when(jnp.logical_not(has_dn))
    def _():
        clear(from_l, n_lev + 2, 2)
        clear(from_r, n_lev + 2, 2)
        clear(eown, n_lev + 2, 2)
        clear(kown, n_lev + 1, 1)
        clear(kx, n_lev + 1, 1)
        clear(adv, n_lev + 2, 2)
        clear(kv, n_lev, 1)

    clear(kown, n_lev + 2, 2)
    clear(awin, n_lev + 4, 2)

    lo8 = lanes(tile) % 16 < 8

    load_bot.wait()
    b = bot[...]
    bown[0] = pack(tiles_of(b), 8)
    bown[1] = pack(tiles_of(b), 4)
    bown[2] = pack(tiles_of(b), 12)

    def edge_masks(b, shifts, strip):
        east, west, north, south = shifts
        top = is_first_row(b.shape, strip)
        end = is_last_row(b.shape, strip)
        bn = jnp.where(end, 0, north(b))
        bs = jnp.where(top, 0, south(b))
        be, bw = east(b), west(b)
        return b, jnp.minimum(b, be), jnp.minimum(b, bn), jnp.minimum(bw, be), jnp.minimum(bs, bn)

    for i, value in enumerate(edge_masks(b, plane_shifts(), False)):
        bmask[i] = value

    chunk = part
    shape = (chunk, 8, LON)

    def pack_levels(step, carry):
        at = step * chunk
        low = lanes(shape) % 16 < 8
        wl = lanes(shape) % 16

        def field(ref, offset):
            return pack([ref[pl.ds(at, chunk), 8 * g : 8 * g + 8, :] for g in range(8)], offset)

        t, s = field(tr.at[0], 8), field(tr.at[1], 8)
        uu, vv = field(u, 8), field(v, 8)
        kref = kx.at[pl.ds(1, n_lev)]
        kl, kr = field(kref, 4), field(kref, 12)
        eown[pl.ds(at + 2, chunk), 0] = t
        eown[pl.ds(at + 2, chunk), 1] = s
        eown[pl.ds(at + 2, chunk), 2] = uu
        eown[pl.ds(at + 2, chunk), 3] = vv
        kown[pl.ds(at + 1, chunk), 0] = kl
        kown[pl.ds(at + 1, chunk), 1] = kr
        msg_r[pl.ds(at, chunk), 0] = jnp.where(low, t, pltpu.roll(s, 8, 2))
        msg_r[pl.ds(at, chunk), 1] = jnp.where(
            wl == 10, pltpu.roll(kr, LON - 1, 2), jnp.where(low, uu, pltpu.roll(vv, 8, 2))
        )
        msg_l[pl.ds(at, chunk), 0] = jnp.where(low, pltpu.roll(s, LON - 8, 2), t)
        msg_l[pl.ds(at, chunk), 1] = jnp.where(
            wl == 5, pltpu.roll(kl, 1, 2), jnp.where(low, pltpu.roll(vv, LON - 8, 2), uu)
        )
        return carry

    for i in range(NQ):
        for copy in loads[i]:
            copy.wait()
        pack_levels(i, 0)

    guests = n_lev // 4
    hosts = n_lev - guests
    slot = lanes((guests, 8, LON)) % 8
    for i in range(2):
        guest_r, guest_l = msg_r[pl.ds(hosts, guests), i], msg_l[pl.ds(hosts, guests), i]
        for j in range(3):
            span = pl.ds(j * guests, guests)
            msg_r[span, i] = jnp.where(slot < 2, pltpu.roll(guest_r, LON - 2 - 2 * j, 2), msg_r[span, i])
            msg_l[span, i] = jnp.where(slot >= 6, pltpu.roll(guest_l, 6 - 2 * j, 2), msg_l[span, i])
    load_kv.wait()

    batch = TB

    def transport(at, count):
        def stack(which):
            return jnp.stack([bmask[which] > first + at + i for i in range(count)], axis=0)

        span = pl.ds(at, count)
        c0, c1 = upwind(tr[0, span], tr[1, span], u[span], v[span], stack(1), stack(2), plane_shifts())
        adv[pl.ds(at + 2, count), 0] = c0
        adv[pl.ds(at + 2, count), 1] = c1

    def transport_ends(step, carry):
        transport(step * (n_lev - 2), 2)
        return carry

    def transport_rest(step, carry):
        transport(2 + step * batch, batch)
        return carry

    lax.fori_loop(0, 2, transport_ends, 0)

    @pl.when(has_up & has_dn)
    def _():
        pl.semaphore_wait(barrier, 8)

    @pl.when(jnp.logical_not(has_up & has_dn))
    def _():
        pl.semaphore_wait(barrier, 5)

    top2, end2 = pl.ds(0, 2), pl.ds(n_lev - 2, 2)
    pre2, post2 = pl.ds(0, 2), pl.ds(n_lev + 2, 2)
    early = (n_lev + 4) // 2 - 2
    first_part, second_part = (0, early), (early, hosts - early)

    def lon_copy(message, target, part, index, device):
        start, count = part
        return remote(message.at[pl.ds(start, count)], target.at[pl.ds(2 + start, count)], index, device)

    lon_1 = [
        lon_copy(msg_r, from_l, first_part, LON_R, (right, dep)),
        lon_copy(msg_l, from_r, first_part, LON_L, (left, dep)),
    ]
    lon_2 = [
        lon_copy(msg_r, from_l, second_part, LON2, (right, dep)),
        lon_copy(msg_l, from_r, second_part, LON2 + 1, (left, dep)),
    ]
    bot_r = remote(bown.at[0], brecv.at[0], BOT_R, (right, dep))
    bot_l = remote(bown.at[0], brecv.at[1], BOT_L, (left, dep))
    ups = [
        remote(msg_r.at[top2], from_l.at[post2], DG_RU, (right, dep - 1)),
        remote(msg_l.at[top2], from_r.at[post2], DG_LU, (left, dep - 1)),
        remote(eown.at[pl.ds(2, 2)], eown.at[post2], E_U, (lon, dep - 1)),
        remote(kown.at[1], kown.at[n_lev + 1], K_U, (lon, dep - 1)),
        remote(kx.at[1], kx.at[n_lev + 1], KX_U, (lon, dep - 1)),
        remote(kv.at[0], kv.at[n_lev], KV_U, (lon, dep - 1)),
        remote(adv.at[pl.ds(2, 2)], adv.at[post2], ADV_U, (lon, dep - 1)),
    ]
    downs = [
        remote(msg_r.at[end2], from_l.at[pre2], DG_RD, (right, dep + 1)),
        remote(msg_l.at[end2], from_r.at[pre2], DG_LD, (left, dep + 1)),
        remote(eown.at[pl.ds(n_lev, 2)], eown.at[pre2], E_D, (lon, dep + 1)),
        remote(kown.at[n_lev], kown.at[0], K_D, (lon, dep + 1)),
        remote(kx.at[n_lev], kx.at[0], KX_D, (lon, dep + 1)),
        remote(adv.at[pl.ds(n_lev, 2)], adv.at[pre2], ADV_D, (lon, dep + 1)),
    ]
    for copy in lon_1:
        copy.start()
    bot_r.start()
    bot_l.start()

    @pl.when(has_up)
    def _():
        for copy in ups[:4] + ups[5:6]:
            copy.start()

    @pl.when(has_dn)
    def _():
        for copy in downs[:4]:
            copy.start()

    for copy in lon_2:
        copy.start()

    lax.fori_loop(0, (n_lev - 4) // batch, transport_rest, 0)

    @pl.when(has_up)
    def _():
        ups[6].start()
        ups[4].start()

    @pl.when(has_dn)
    def _():
        downs[5].start()
        downs[4].start()


    def flux_levels(at, count):
        _, _, north, south = plane_shifts()
        for i in [at + i for i in range(count)]:
            k = first + i - 1
            kw = jnp.where(k < 0, FAR, k)
            kz = jnp.where(k < 1, FAR, k + 1)
            mid = [adv[i + 1, n] for n in range(2)]
            norths, souths = [north(c) for c in mid], [south(c) for c in mid]
            parts = []
            for g in range(8):
                cut = slice(8 * g, 8 * g + 8)
                bottom = bmask[0, cut]
                parts.append(fluxes(
                    [adv[i, n, cut] for n in range(2)], [c[cut] for c in mid], [adv[i + 2, n, cut] for n in range(2)],
                    [c[cut] for c in norths], [c[cut] for c in souths],
                    jnp.where(bottom > kw, 0.25 * kx[i, cut], 0.0),
                    bmask[3, cut] > kw, bmask[4, cut] > kw, bottom > kz,
                ))
            for n in range(2):
                side = jnp.concatenate([part[1][n] for part in parts], axis=0)
                flat[i, n] = jnp.concatenate([part[0][n] for part in parts], axis=0) + (north(side) - south(side))
                vert[i, n] = jnp.concatenate([part[2][n] for part in parts], axis=0)

    def flux_rest(step, carry):
        flux_levels(2 + FB * step, FB)
        return carry

    def flux_ends(step, carry):
        flux_levels(step * n_lev, 2)
        return carry

    lax.fori_loop(0, (n_lev - 2) // FB, flux_rest, 0)

    @pl.when(has_dn)
    def _():
        ups[5].wait_recv()

    def e_of(at):
        k = first + at
        k = jnp.where(k < 1, FAR, k)
        return jnp.where(bmask[0] > k, kv[at], 0.0)

    def eliminate(at, carry):
        ratio, prod, spike, p_top, e_here = carry
        e_next = e_of(at + 1)
        recip = 1.0 / (1.0 + e_next + e_here * (1.0 - ratio))
        gain = e_here * recip
        inv[at] = recip
        gdn[at] = gain
        rprod[at] = prod
        ratio = e_next * recip
        rdn[at] = ratio
        spike = spike * gain
        pspk[at] = spike
        p_top = p_top + prod * spike
        return ratio, prod * ratio, spike, p_top, e_next

    zero, one = jnp.zeros(plane, jnp.float32), jnp.ones(plane, jnp.float32)
    _, q_top, p_end, p_top, _ = lax.fori_loop(
        0, n_lev, eliminate, (zero, one, one, zero, e_of(0))
    )
    send_end[0, 0] = p_top
    send_end[0, 1] = p_end
    send_end[1, 0] = q_top
    send_end[1, 1] = rdn[n_lev - 1]
    z_copy = remote(send_end.at[i_end, i_end], zmat, ZM, (lon, in_dev))
    q_copy = remote(qmat, qpart, QM, (lon, 3 - dep))

    @pl.when(outer)
    def _():
        z_copy.start()


    def pack_windows(at, count):
        low = lanes((count, 8, LON)) % 16 < 8
        for n in range(2):
            parts = [adv[pl.ds(at, count), n, 8 * g : 8 * g + 8, :] for g in range(8)]
            gwin[n, pl.ds(at, count)] = jnp.where(low, pack(parts, 12), pack(parts, 4))

    def pack_own(step, carry):
        pack_windows(2 + step * (n_lev // 2), n_lev // 2)
        return carry

    lax.fori_loop(0, 2, pack_own, 0)

    bot_r.wait_recv()
    bot_l.wait_recv()
    for copy in lon_1:
        copy.wait_recv()

    @pl.when(has_dn)
    def _():
        for copy in ups[:4]:
            copy.wait_recv()

    @pl.when(has_up)
    def _():
        for copy in downs[:4]:
            copy.wait_recv()

    b_l = jnp.where(lo8, brecv[0], bown[0])
    b_r = jnp.where(lo8, bown[0], brecv[1])
    w_l = jnp.where(lo8, pltpu.roll(b_l, LON - 4, 1), bown[1])
    w_r = jnp.where(lo8, bown[2], pltpu.roll(b_r, 4, 1))
    for side, value in enumerate((b_l, b_r)):
        masks = edge_masks(value, strip_shifts(), True)
        bstrip[0, side] = masks[1]
        bstrip[1, side] = masks[2]
    for side, value in enumerate((w_l, w_r)):
        masks = edge_masks(value, strip_shifts(), True)
        bstrip[2, side] = masks[0]
        bstrip[3, side] = masks[3]
        bstrip[4, side] = masks[4]

    chunk = (n_lev + 4) // 2
    shape = (chunk, 8, LON)
    flatshape = (2 * chunk, 8, LON)

    def level_mask(which, start, floor, shift):
        parts = []
        for i in range(chunk):
            k = start + i
            k = jnp.where(k < floor, FAR, k + shift)
            parts.append(bstrip[which] > k)
        return jnp.concatenate(parts, axis=0)

    def join(left_part, right_part):
        return jnp.stack([left_part, right_part], axis=1).reshape(flatshape)

    def strip_transport(step, carry):
        at = step * chunk
        k = first + at - 2
        low = lanes(shape) % 16 < 8
        own = [eown[pl.ds(at, chunk), i] for i in range(4)]
        la, lb = from_l[pl.ds(at, chunk), 0], from_l[pl.ds(at, chunk), 1]
        ra, rb = from_r[pl.ds(at, chunk), 0], from_r[pl.ds(at, chunk), 1]

        def assemble(i, from_left, from_right):
            return join(jnp.where(low, from_left, own[i]), jnp.where(low, own[i], from_right))

        c0 = assemble(0, la, ra)
        c1 = assemble(1, pltpu.roll(la, LON - 8, 2), pltpu.roll(ra, 8, 2))
        uu = assemble(2, lb, rb)
        vv = assemble(3, pltpu.roll(lb, LON - 8, 2), pltpu.roll(rb, 8, 2))
        done = upwind(c0, c1, uu, vv, level_mask(0, k, 0, 0), level_mask(1, k, 0, 0), strip_shifts())
        for n in range(2):
            both = done[n].reshape(chunk, 2, 8, LON)
            g = gwin[n, pl.ds(at, chunk)]
            awin[pl.ds(at, chunk), n, 0] = jnp.where(low, pltpu.roll(both[:, 0], LON - 4, 2), g)
            awin[pl.ds(at, chunk), n, 1] = jnp.where(low, g, pltpu.roll(both[:, 1], 4, 2))
        return carry

    strip_transport(0, 0)
    for copy in lon_2:
        copy.wait_recv()
    for i in range(2):
        guest_l = guest_r = None
        for j in range(3):
            span = pl.ds(2 + j * guests, guests)
            part_l = pltpu.roll(from_l[span, i], 2 + 2 * j, 2)
            part_r = pltpu.roll(from_r[span, i], LON - 6 + 2 * j, 2)
            guest_l = part_l if j == 0 else jnp.where(slot >= 2 + 2 * j, part_l, guest_l)
            guest_r = part_r if j == 0 else jnp.where(slot >= 2 * j, part_r, guest_r)
        from_l[pl.ds(2 + hosts, guests), i] = guest_l
        from_r[pl.ds(2 + hosts, guests), i] = guest_r

    strip_transport(1, 0)

    @pl.when(has_dn)
    def _():
        ups[4].wait_recv()
        ups[6].wait_recv()

    @pl.when(has_up)
    def _():
        downs[4].wait_recv()
        downs[5].wait_recv()

    lax.fori_loop(0, 2, flux_ends, 0)

    low2 = lanes((2, 8, LON)) % 16 < 8
    for at in (0, n_lev + 2):
        pack_windows(at, 2)
        for n in range(2):
            g = gwin[n, pl.ds(at, 2)]
            awin[pl.ds(at, 2), n, 0] = jnp.where(low2, awin[pl.ds(at, 2), n, 0], g)
            awin[pl.ds(at, 2), n, 1] = jnp.where(low2, g, awin[pl.ds(at, 2), n, 1])

    @pl.when(inner)
    def _():
        z_copy.wait_recv()
        z = zmat[...]
        inv_t = 1.0 / (1.0 - z * send_end[o_end, o_end])
        tmat[0] = inv_t
        beta = z * send_end[i_end, o_end] * inv_t
        tmat[1] = beta
        qmat[...] = send_end[i_end, i_end] + send_end[o_end, i_end] * beta
        q_copy.start()


    chunk = FC
    shape = (chunk, 8, LON)
    flatshape = (2 * chunk, 8, LON)

    def strip_flux(step, carry):
        at = step * chunk
        k = first + at - 1
        wl = lanes(shape) % 16
        lb, rb = from_l[pl.ds(at + 1, chunk), 1], from_r[pl.ds(at + 1, chunk), 1]
        kl = jnp.where(wl == 3, pltpu.roll(lb, LON - 7, 2), kown[pl.ds(at, chunk), 0])
        kr = jnp.where(wl == 12, pltpu.roll(rb, 7, 2), kown[pl.ds(at, chunk), 1])
        kappa = jnp.where(level_mask(2, k, 0, 0), 0.25 * join(kl, kr), 0.0)

        def window(shift):
            return [awin[pl.ds(at + shift, chunk), n].reshape(flatshape) for n in range(2)]

        _, _, north, south = strip_shifts()
        mid = window(1)
        f, y, w = fluxes(
            window(0), mid, window(2), [north(c) for c in mid], [south(c) for c in mid], kappa,
            level_mask(3, k, 0, 0), level_mask(4, k, 0, 0), level_mask(2, k, 1, 1),
        )
        for n in range(2):
            sflat[pl.ds(at, chunk), n] = (f[n] + (north(y[n]) - south(y[n]))).reshape(chunk, 2, 8, LON)
            svert[pl.ds(at, chunk), n] = w[n].reshape(chunk, 2, 8, LON)
        return carry

    lax.fori_loop(0, (n_lev + 4) // chunk, strip_flux, 0)

    chunk = n_lev
    shape = (chunk, 8, LON)
    flatshape = (2 * chunk, 8, LON)

    def strip_update(step, carry):
        at = step * chunk
        low = lanes(shape) % 16 < 8
        wet = level_mask(2, first + at, 0, 0)
        for n in range(2):
            gain = (
                sflat[pl.ds(at + 1, chunk), n] + svert[pl.ds(at + 2, chunk), n] - svert[pl.ds(at, chunk), n]
            ).reshape(flatshape)
            new = awin[pl.ds(at + 2, chunk), n].reshape(flatshape) + jnp.where(wet, gain, 0.0)
            both = new.reshape(chunk, 2, 8, LON)
            edge[pl.ds(at, chunk), n] = jnp.where(
                low, pltpu.roll(both[:, 1], LON - 4, 2), pltpu.roll(both[:, 0], 4, 2)
            )
        return carry

    lax.fori_loop(0, n_lev // chunk, strip_update, 0)

    yend[...] = jnp.zeros(yend.shape, jnp.float32)
    fval[0] = jnp.zeros((2,) + plane, jnp.float32)
    lane = lanes(plane)
    on_edge = (lane < 6) | (lane >= LON - 6)

    group = 4

    def way_down(n, step, carry):
        at = step * group
        value, total = fval[at, n], yend[0, n]
        for i in range(group):
            here = at + i
            wet = bmask[0] > first + here
            new = adv[here + 2, n] + jnp.where(wet, flat[here + 1, n] + vert[here + 2, n] - vert[here, n], 0.0)
            packed = edge[here, n]
            fixed = jnp.concatenate(
                [pltpu.roll(packed, (LON - 8 - 16 * g) % LON, 1) for g in range(8)], axis=0
            )
            new = jnp.where(on_edge, fixed, new)
            value = new * inv[here] + gdn[here] * value
            fval[here + 1, n] = value
            total = total + rprod[here] * value
        yend[0, n] = total
        return carry

    z_val = [remote(yend.at[i_end, n], zval.at[n], ZV + n, (lon, in_dev)) for n in range(2)]
    y_val = [remote(yval.at[n], ypart.at[n], YV + n, (lon, 3 - dep)) for n in range(2)]
    x_val = [remote(xout.at[n], xend.at[i_end, n], XO + n, (lon, out_dev)) for n in range(2)]

    for n in range(2):
        lax.fori_loop(0, n_lev // group, functools.partial(way_down, n), 0)
        yend[1, n] = fval[n_lev, n]

        @pl.when(outer)
        def _():
            z_val[n].start()

    @pl.when(outer)
    def _():
        xend[o_end] = jnp.zeros((2,) + plane, jnp.float32)

    @pl.when(inner)
    def _():
        for n in range(2):
            z_val[n].wait_recv()
            alpha = (zval[n] + zmat[...] * yend[o_end, n]) * tmat[0]
            xend[o_end, n] = alpha
            yval[n] = yend[i_end, n] + send_end[o_end, i_end] * alpha
            y_val[n].start()

    def back_matrix(step, carry):
        p_low, q_low = carry
        at = n_lev - 1 - step
        ratio = rdn[at]
        p = pspk[at] + ratio * p_low
        q = ratio * q_low
        pspk[at] = p
        qspk[at] = q
        return p, q

    lax.fori_loop(0, n_lev, back_matrix, (zero, one))

    def way_up(step, carry):
        at = n_lev - 1 - step
        ratio = rdn[at - 1]
        for n in range(2):
            fval[at, n] = fval[at, n] + ratio * fval[at + 1, n]
        return carry

    lax.fori_loop(0, n_lev - 1, way_up, 0)

    @pl.when(inner)
    def _():
        q_copy.wait_recv()
        q_other = qpart[...]
        inv_m = 1.0 / (1.0 - q_other * qmat[...])
        for n in range(2):
            y_val[n].wait_recv()
            x_in = (ypart[n] + q_other * yval[n]) * inv_m
            xout[n] = (yend[o_end, n] + send_end[o_end, o_end] * zval[n] + send_end[i_end, o_end] * x_in) * tmat[0]
            x_val[n].start()
            xend[i_end, n] = x_in
            xend[o_end, n] = xend[o_end, n] + tmat[1] * x_in

    @pl.when(outer)
    def _():
        for copy in x_val:
            copy.wait_recv()

    part = n_lev // 4
    for i in range(4):
        def finish(at, carry):
            p, q = pspk[at], qspk[at]
            for n in range(2):
                out_hbm[n, at] = fval[at + 1, n] + p * xend[0, n] + q * xend[1, n]
            return carry

        lax.fori_loop(i * part, (i + 1) * part, finish, 0)

    for copy in lon_1 + lon_2 + [bot_r, bot_l]:
        copy.wait_send()

    @pl.when(has_up)
    def _():
        for copy in ups:
            copy.wait_send()

    @pl.when(has_dn)
    def _():
        for copy in downs:
            copy.wait_send()

    @pl.when(outer)
    def _():
        z_copy.wait_send()
        for copy in z_val:
            copy.wait_send()

    @pl.when(inner)
    def _():
        q_copy.wait_send()
        for copy in y_val + x_val:
            copy.wait_send()


def per_device(n_lon, n_dep, tracers, u_east, v_north, kappa_h, kappa_v, bottom):
    n_lev = tracers.shape[1]
    ext = n_lev + 4

    def f32(*shape):
        return pltpu.VMEM(shape, jnp.float32)

    def i32(*shape):
        return pltpu.VMEM(shape, jnp.int32)

    scratch = [
        f32(2, n_lev, LAT, LON), f32(n_lev, LAT, LON), f32(n_lev, LAT, LON),
        f32(n_lev + 2, LAT, LON), f32(n_lev + 1, LAT, LON), i32(LAT, LON),
        i32(5, LAT, LON), i32(5, 2, 8, LON), i32(3, 8, LON), i32(2, 8, LON),
        f32(ext, 4, 8, LON), f32(ext, 2, 8, LON),
        f32(n_lev, 2, 8, LON), f32(n_lev, 2, 8, LON),
        f32(ext + 1, 2, 8, LON), f32(ext + 1, 2, 8, LON),
        f32(ext, 2, LAT, LON), f32(n_lev + 2, 2, LAT, LON), f32(n_lev + 2, 2, LAT, LON),
        f32(2, ext, 8, LON), f32(ext + 2, 2, 2, 8, LON),
        f32(ext, 2, 2, 8, LON), f32(ext, 2, 2, 8, LON), f32(n_lev, 2, 8, LON),
    ]
    scratch += [f32(n_lev, LAT, LON)] * 6
    scratch += [
        f32(n_lev + 1, 2, LAT, LON), f32(2, 2, LAT, LON), f32(2, 2, LAT, LON),
        f32(LAT, LON), f32(LAT, LON), f32(LAT, LON),
        f32(2, LAT, LON), f32(2, LAT, LON), f32(2, LAT, LON), f32(2, LAT, LON),
        f32(2, 2, LAT, LON), f32(2, LAT, LON),
        pltpu.SemaphoreType.DMA((4 * NQ + 2,)),
        pltpu.SemaphoreType.DMA((N_COPIES,)), pltpu.SemaphoreType.DMA((N_COPIES,)),
    ]
    hbm = pl.BlockSpec(memory_space=pltpu.HBM)
    return pl.pallas_call(
        functools.partial(kernel, n_lon, n_dep, n_lev),
        out_shape=jax.ShapeDtypeStruct(tracers.shape, jnp.float32),
        in_specs=[hbm] * 6,
        out_specs=pl.BlockSpec(memory_space=pltpu.VMEM),
        scratch_shapes=scratch,
        name="tracer_step",
        compiler_params=pltpu.CompilerParams(
            collective_id=0, has_side_effects=True, vmem_limit_bytes=48 << 20
        ),
    )(*(pltpu.with_memory_space_constraint(a, pltpu.HBM) for a in (tracers, u_east, v_north, kappa_h, kappa_v, bottom)))


def solution(mesh):
    n_lon, n_dep = mesh.shape["lon"], mesh.shape["dep"]
    level = P("dep", None, "lon")
    return jax.shard_map(
        functools.partial(per_device, n_lon, n_dep),
        mesh=mesh,
        in_specs=(P(None, "dep", None, "lon"), level, level, level, level, P(None, "lon")),
        out_specs=P(None, "dep", None, "lon"),
        check_vma=False,
    )
```

```python
import functools

import jax
import jax.numpy as jnp
from jax import lax
from jax.experimental import pallas as pl
from jax.experimental.pallas import tpu as pltpu
from jax.sharding import PartitionSpec as P

MESH = pl.DeviceIdType.MESH
SUB = 4
LAT = 64
LON = 128
THERMAL = 0.2
HALINE = 0.8
FAR = 1 << 20
TB, FB, FC, NQ = 4, 2, 12, 2

(LON_R, LON_L, BOT_R, BOT_L, DG_RU, DG_RD, DG_LU, DG_LD, E_U, E_D, K_U, K_D, KX_U, KX_D, KV_U, ADV_U, ADV_D, ZM, QM) = range(19)
ZV, YV, XO, LON2 = 19, 21, 23, 25
N_COPIES = 27


def lanes(shape):
    return lax.broadcasted_iota(jnp.int32, shape, len(shape) - 1)


def rows(shape):
    return lax.broadcasted_iota(jnp.int32, shape, len(shape) - 2)


def plane_shifts():
    def east(x):
        return pltpu.roll(x, LON - 1, x.ndim - 1)

    def west(x):
        return pltpu.roll(x, 1, x.ndim - 1)

    def north(x):
        return pltpu.roll(x, LAT - 1, x.ndim - 2)

    def south(x):
        return pltpu.roll(x, 1, x.ndim - 2)

    return east, west, north, south


def strip_shifts():
    def east(x):
        return pltpu.roll(x, LON - 1, x.ndim - 1)

    def west(x):
        return pltpu.roll(x, 1, x.ndim - 1)

    def north(x):
        y = pltpu.roll(x, 7, x.ndim - 2)
        return jnp.where(rows(x.shape) == 7, pltpu.roll(y, 112, x.ndim - 1), y)

    def south(x):
        y = pltpu.roll(x, 1, x.ndim - 2)
        return jnp.where(rows(x.shape) == 0, pltpu.roll(y, 16, x.ndim - 1), y)

    return east, west, north, south


def is_first_row(shape, strip):
    if strip:
        return (rows(shape) == 0) & (lanes(shape) < 16)
    return rows(shape) == 0


def is_last_row(shape, strip):
    if strip:
        return (rows(shape) == 7) & (lanes(shape) >= 112)
    return rows(shape) == LAT - 1


def upwind(c0, c1, u, v, face_x, face_y, shifts):
    east, west, north, south = shifts
    u = jnp.where(face_x, u, 0.0)
    v = jnp.where(face_y, v, 0.0)
    up = jnp.maximum(u, 0.0)
    vp = jnp.maximum(v, 0.0)
    ce = up - u
    cn = vp - v
    cw = west(up)
    cs = south(vp)
    keep = 1.0 - up - vp - west(ce) - south(cn)

    def advance(c):
        return keep * c + cw * west(c) + ce * east(c) + cs * south(c) + cn * north(c)

    for _ in range(SUB):
        c0 = advance(c0)
        c1 = advance(c1)
    return c0, c1


def fluxes(low, mid, high, north, south, kappa, mask_x, mask_y, mask_z):
    def east(x):
        return pltpu.roll(x, LON - 1, x.ndim - 1)

    def west(x):
        return pltpu.roll(x, 1, x.ndim - 1)

    gx = [jnp.where(mask_x, east(c) - west(c), 0.0) for c in mid]
    gy = [jnp.where(mask_y, a - b, 0.0) for a, b in zip(north, south)]
    gz = [jnp.where(mask_z, a - b, 0.0) for a, b in zip(high, low)]
    rx, ry, rz = (g[1] - (THERMAL / HALINE) * g[0] for g in (gx, gy, gz))
    ratio = rz / ((4.0 / HALINE**2) + rx * rx + ry * ry + rz * rz)
    sx, sy = rx * ratio, ry * ratio
    flat, side, vert = [], [], []
    for n in range(2):
        fx = kappa * (gx[n] + sx * gz[n])
        fy = kappa * (gy[n] + sy * gz[n])
        vert.append(sx * fx + sy * fy)
        flat.append(east(fx) - west(fx))
        side.append(fy)
    return flat, side, vert


def pack(tiles, offset):
    group = lanes(tiles[0].shape) // 16
    out = None
    for g in range(8):
        moved = pltpu.roll(tiles[g], (16 * g + offset) % LON, tiles[g].ndim - 1)
        out = moved if out is None else jnp.where(group == g, moved, out)
    return out


def tiles_of(plane):
    return [plane[..., 8 * g : 8 * g + 8, :] for g in range(8)]


def kernel(
    n_lon, n_dep, n_lev,
    tr_hbm, u_hbm, v_hbm, kh_hbm, kv_hbm, bot_hbm,
    out_hbm,
    tr, u, v, kx, kv, bot,
    bmask, bstrip, bown, brecv,
    eown, kown, msg_r, msg_l, from_l, from_r,
    adv, flat, vert, gwin, awin, sflat, svert, edge,
    inv, gdn, rdn, rprod, pspk, qspk, fval, yend, send_end,
    zmat, qmat, qpart, zval, yval, ypart, xout, xend, tmat,
    in_sem, ssem, rsem,
):
    lon = lax.axis_index("lon")
    dep = lax.axis_index("dep")
    right = lax.rem(lon + 1, n_lon)
    left = lax.rem(lon + n_lon - 1, n_lon)
    first = dep * n_lev
    has_up = dep > 0
    has_dn = dep < n_dep - 1
    inner = (dep == 1) | (dep == 2)
    outer = jnp.logical_not(inner)
    o_end = jnp.where(dep < 2, 0, 1)
    i_end = 1 - o_end
    out_dev = jnp.where(dep < 2, 0, 3)
    in_dev = jnp.where(dep < 2, 1, 2)
    plane = (LAT, LON)
    tile = (8, LON)

    def remote(src, dst, index, device):
        return pltpu.make_async_remote_copy(
            src_ref=src, dst_ref=dst, send_sem=ssem.at[index], recv_sem=rsem.at[index],
            device_id=device, device_id_type=MESH,
        )

    part = n_lev // NQ
    load_bot = pltpu.make_async_copy(bot_hbm, bot, in_sem.at[0])
    load_kv = pltpu.make_async_copy(kv_hbm, kv.at[pl.ds(0, n_lev)], in_sem.at[1])
    load_bot.start()
    loads = []
    for i in range(NQ):
        span = pl.ds(i * part, part)
        loads.append([
            pltpu.make_async_copy(tr_hbm.at[:, span], tr.at[:, span], in_sem.at[4 * i + 2]),
            pltpu.make_async_copy(u_hbm.at[span], u.at[span], in_sem.at[4 * i + 3]),
            pltpu.make_async_copy(v_hbm.at[span], v.at[span], in_sem.at[4 * i + 4]),
            pltpu.make_async_copy(kh_hbm.at[span], kx.at[pl.ds(1 + i * part, part)], in_sem.at[4 * i + 5]),
        ])
        for copy in loads[-1]:
            copy.start()
    load_kv.start()

    barrier = pltpu.get_barrier_semaphore()

    def greet(device):
        pl.semaphore_signal(barrier, inc=1, device_id=device, device_id_type=MESH)

    greet((right, dep))
    greet((left, dep))

    @pl.when(has_up)
    def _():
        greet((lon, dep - 1))
        greet((right, dep - 1))
        greet((left, dep - 1))

    @pl.when(has_dn)
    def _():
        greet((lon, dep + 1))
        greet((right, dep + 1))
        greet((left, dep + 1))

    def clear(ref, start, count):
        part = ref.at[pl.ds(start, count)]
        part[...] = jnp.zeros(part.shape, part.dtype)

    @pl.when(jnp.logical_not(has_up))
    def _():
        clear(from_l, 0, 2)
        clear(from_r, 0, 2)
        clear(eown, 0, 2)
        clear(kown, 0, 1)
        clear(kx, 0, 1)
        clear(adv, 0, 2)

    @pl.when(jnp.logical_not(has_dn))
    def _():
        clear(from_l, n_lev + 2, 2)
        clear(from_r, n_lev + 2, 2)
        clear(eown, n_lev + 2, 2)
        clear(kown, n_lev + 1, 1)
        clear(kx, n_lev + 1, 1)
        clear(adv, n_lev + 2, 2)
        clear(kv, n_lev, 1)

    clear(kown, n_lev + 2, 2)
    clear(awin, n_lev + 4, 2)

    lo8 = lanes(tile) % 16 < 8

    load_bot.wait()
    b = bot[...]
    bown[0] = pack(tiles_of(b), 8)
    bown[1] = pack(tiles_of(b), 4)
    bown[2] = pack(tiles_of(b), 12)

    def edge_masks(b, shifts, strip):
        east, west, north, south = shifts
        top = is_first_row(b.shape, strip)
        end = is_last_row(b.shape, strip)
        bn = jnp.where(end, 0, north(b))
        bs = jnp.where(top, 0, south(b))
        be, bw = east(b), west(b)
        return b, jnp.minimum(b, be), jnp.minimum(b, bn), jnp.minimum(bw, be), jnp.minimum(bs, bn)

    for i, value in enumerate(edge_masks(b, plane_shifts(), False)):
        bmask[i] = value

    chunk = part
    shape = (chunk, 8, LON)

    def pack_levels(step, carry):
        at = step * chunk
        low = lanes(shape) % 16 < 8
        wl = lanes(shape) % 16

        def field(ref, offset):
            return pack([ref[pl.ds(at, chunk), 8 * g : 8 * g + 8, :] for g in range(8)], offset)

        t, s = field(tr.at[0], 8), field(tr.at[1], 8)
        uu, vv = field(u, 8), field(v, 8)
        kref = kx.at[pl.ds(1, n_lev)]
        kl, kr = field(kref, 4), field(kref, 12)
        eown[pl.ds(at + 2, chunk), 0] = t
        eown[pl.ds(at + 2, chunk), 1] = s
        eown[pl.ds(at + 2, chunk), 2] = uu
        eown[pl.ds(at + 2, chunk), 3] = vv
        kown[pl.ds(at + 1, chunk), 0] = kl
        kown[pl.ds(at + 1, chunk), 1] = kr
        msg_r[pl.ds(at, chunk), 0] = jnp.where(low, t, pltpu.roll(s, 8, 2))
        msg_r[pl.ds(at, chunk), 1] = jnp.where(
            wl == 10, pltpu.roll(kr, LON - 1, 2), jnp.where(low, uu, pltpu.roll(vv, 8, 2))
        )
        msg_l[pl.ds(at, chunk), 0] = jnp.where(low, pltpu.roll(s, LON - 8, 2), t)
        msg_l[pl.ds(at, chunk), 1] = jnp.where(
            wl == 5, pltpu.roll(kl, 1, 2), jnp.where(low, pltpu.roll(vv, LON - 8, 2), uu)
        )
        return carry

    for i in range(NQ):
        for copy in loads[i]:
            copy.wait()
        pack_levels(i, 0)

    guests = n_lev // 4
    hosts = n_lev - guests
    slot = lanes((guests, 8, LON)) % 8
    for i in range(2):
        guest_r, guest_l = msg_r[pl.ds(hosts, guests), i], msg_l[pl.ds(hosts, guests), i]
        for j in range(3):
            span = pl.ds(j * guests, guests)
            msg_r[span, i] = jnp.where(slot < 2, pltpu.roll(guest_r, LON - 2 - 2 * j, 2), msg_r[span, i])
            msg_l[span, i] = jnp.where(slot >= 6, pltpu.roll(guest_l, 6 - 2 * j, 2), msg_l[span, i])
    load_kv.wait()

    batch = TB

    def transport(at, count):
        def stack(which):
            return jnp.stack([bmask[which] > first + at + i for i in range(count)], axis=0)

        span = pl.ds(at, count)
        c0, c1 = upwind(tr[0, span], tr[1, span], u[span], v[span], stack(1), stack(2), plane_shifts())
        adv[pl.ds(at + 2, count), 0] = c0
        adv[pl.ds(at + 2, count), 1] = c1

    def transport_ends(step, carry):
        transport(step * (n_lev - 2), 2)
        return carry

    def transport_rest(step, carry):
        transport(2 + step * batch, batch)
        return carry

    lax.fori_loop(0, 2, transport_ends, 0)

    @pl.when(has_up & has_dn)
    def _():
        pl.semaphore_wait(barrier, 8)

    @pl.when(jnp.logical_not(has_up & has_dn))
    def _():
        pl.semaphore_wait(barrier, 5)

    top2, end2 = pl.ds(0, 2), pl.ds(n_lev - 2, 2)
    pre2, post2 = pl.ds(0, 2), pl.ds(n_lev + 2, 2)
    early = (n_lev + 4) // 2 - 2
    first_part, second_part = (0, early), (early, hosts - early)

    def lon_copy(message, target, part, index, device):
        start, count = part
        return remote(message.at[pl.ds(start, count)], target.at[pl.ds(2 + start, count)], index, device)

    lon_1 = [
        lon_copy(msg_r, from_l, first_part, LON_R, (right, dep)),
        lon_copy(msg_l, from_r, first_part, LON_L, (left, dep)),
    ]
    lon_2 = [
        lon_copy(msg_r, from_l, second_part, LON2, (right, dep)),
        lon_copy(msg_l, from_r, second_part, LON2 + 1, (left, dep)),
    ]
    bot_r = remote(bown.at[0], brecv.at[0], BOT_R, (right, dep))
    bot_l = remote(bown.at[0], brecv.at[1], BOT_L, (left, dep))
    ups = [
        remote(msg_r.at[top2], from_l.at[post2], DG_RU, (right, dep - 1)),
        remote(msg_l.at[top2], from_r.at[post2], DG_LU, (left, dep - 1)),
        remote(eown.at[pl.ds(2, 2)], eown.at[post2], E_U, (lon, dep - 1)),
        remote(kown.at[1], kown.at[n_lev + 1], K_U, (lon, dep - 1)),
        remote(kx.at[1], kx.at[n_lev + 1], KX_U, (lon, dep - 1)),
        remote(kv.at[0], kv.at[n_lev], KV_U, (lon, dep - 1)),
        remote(adv.at[pl.ds(2, 2)], adv.at[post2], ADV_U, (lon, dep - 1)),
    ]
    downs = [
        remote(msg_r.at[end2], from_l.at[pre2], DG_RD, (right, dep + 1)),
        remote(msg_l.at[end2], from_r.at[pre2], DG_LD, (left, dep + 1)),
        remote(eown.at[pl.ds(n_lev, 2)], eown.at[pre2], E_D, (lon, dep + 1)),
        remote(kown.at[n_lev], kown.at[0], K_D, (lon, dep + 1)),
        remote(kx.at[n_lev], kx.at[0], KX_D, (lon, dep + 1)),
        remote(adv.at[pl.ds(n_lev, 2)], adv.at[pre2], ADV_D, (lon, dep + 1)),
    ]
    for copy in lon_1:
        copy.start()
    bot_r.start()
    bot_l.start()

    @pl.when(has_up)
    def _():
        for copy in ups[:4] + ups[5:6]:
            copy.start()

    @pl.when(has_dn)
    def _():
        for copy in downs[:4]:
            copy.start()

    for copy in lon_2:
        copy.start()

    lax.fori_loop(0, (n_lev - 4) // batch, transport_rest, 0)

    @pl.when(has_up)
    def _():
        ups[6].start()
        ups[4].start()

    @pl.when(has_dn)
    def _():
        downs[5].start()
        downs[4].start()


    def flux_levels(at, count):
        _, _, north, south = plane_shifts()
        for i in [at + i for i in range(count)]:
            k = first + i - 1
            kw = jnp.where(k < 0, FAR, k)
            kz = jnp.where(k < 1, FAR, k + 1)
            mid = [adv[i + 1, n] for n in range(2)]
            norths, souths = [north(c) for c in mid], [south(c) for c in mid]
            parts = []
            for g in range(8):
                cut = slice(8 * g, 8 * g + 8)
                bottom = bmask[0, cut]
                parts.append(fluxes(
                    [adv[i, n, cut] for n in range(2)], [c[cut] for c in mid], [adv[i + 2, n, cut] for n in range(2)],
                    [c[cut] for c in norths], [c[cut] for c in souths],
                    jnp.where(bottom > kw, 0.25 * kx[i, cut], 0.0),
                    bmask[3, cut] > kw, bmask[4, cut] > kw, bottom > kz,
                ))
            for n in range(2):
                side = jnp.concatenate([part[1][n] for part in parts], axis=0)
                flat[i, n] = jnp.concatenate([part[0][n] for part in parts], axis=0) + (north(side) - south(side))
                vert[i, n] = jnp.concatenate([part[2][n] for part in parts], axis=0)

    def flux_rest(step, carry):
        flux_levels(2 + FB * step, FB)
        return carry

    def flux_ends(step, carry):
        flux_levels(step * n_lev, 2)
        return carry

    lax.fori_loop(0, (n_lev - 2) // FB, flux_rest, 0)

    @pl.when(has_dn)
    def _():
        ups[5].wait_recv()

    def e_of(at):
        k = first + at
        k = jnp.where(k < 1, FAR, k)
        return jnp.where(bmask[0] > k, kv[at], 0.0)

    def eliminate(at, carry):
        ratio, prod, spike, p_top, e_here = carry
        e_next = e_of(at + 1)
        recip = 1.0 / (1.0 + e_next + e_here * (1.0 - ratio))
        gain = e_here * recip
        inv[at] = recip
        gdn[at] = gain
        rprod[at] = prod
        ratio = e_next * recip
        rdn[at] = ratio
        spike = spike * gain
        pspk[at] = spike
        p_top = p_top + prod * spike
        return ratio, prod * ratio, spike, p_top, e_next

    zero, one = jnp.zeros(plane, jnp.float32), jnp.ones(plane, jnp.float32)
    _, q_top, p_end, p_top, _ = lax.fori_loop(
        0, n_lev, eliminate, (zero, one, one, zero, e_of(0))
    )
    send_end[0, 0] = p_top
    send_end[0, 1] = p_end
    send_end[1, 0] = q_top
    send_end[1, 1] = rdn[n_lev - 1]
    z_copy = remote(send_end.at[i_end, i_end], zmat, ZM, (lon, in_dev))
    q_copy = remote(qmat, qpart, QM, (lon, 3 - dep))

    @pl.when(outer)
    def _():
        z_copy.start()


    def pack_windows(at, count):
        low = lanes((count, 8, LON)) % 16 < 8
        for n in range(2):
            parts = [adv[pl.ds(at, count), n, 8 * g : 8 * g + 8, :] for g in range(8)]
            gwin[n, pl.ds(at, count)] = jnp.where(low, pack(parts, 12), pack(parts, 4))

    def pack_own(step, carry):
        pack_windows(2 + step * (n_lev // 2), n_lev // 2)
        return carry

    lax.fori_loop(0, 2, pack_own, 0)

    bot_r.wait_recv()
    bot_l.wait_recv()
    for copy in lon_1:
        copy.wait_recv()

    @pl.when(has_dn)
    def _():
        for copy in ups[:4]:
            copy.wait_recv()

    @pl.when(has_up)
    def _():
        for copy in downs[:4]:
            copy.wait_recv()

    b_l = jnp.where(lo8, brecv[0], bown[0])
    b_r = jnp.where(lo8, bown[0], brecv[1])
    w_l = jnp.where(lo8, pltpu.roll(b_l, LON - 4, 1), bown[1])
    w_r = jnp.where(lo8, bown[2], pltpu.roll(b_r, 4, 1))
    for side, value in enumerate((b_l, b_r)):
        masks = edge_masks(value, strip_shifts(), True)
        bstrip[0, side] = masks[1]
        bstrip[1, side] = masks[2]
    for side, value in enumerate((w_l, w_r)):
        masks = edge_masks(value, strip_shifts(), True)
        bstrip[2, side] = masks[0]
        bstrip[3, side] = masks[3]
        bstrip[4, side] = masks[4]

    chunk = (n_lev + 4) // 2
    shape = (chunk, 8, LON)
    flatshape = (2 * chunk, 8, LON)

    def level_mask(which, start, floor, shift):
        parts = []
        for i in range(chunk):
            k = start + i
            k = jnp.where(k < floor, FAR, k + shift)
            parts.append(bstrip[which] > k)
        return jnp.concatenate(parts, axis=0)

    def join(left_part, right_part):
        return jnp.stack([left_part, right_part], axis=1).reshape(flatshape)

    def strip_transport(step, carry):
        at = step * chunk
        k = first + at - 2
        low = lanes(shape) % 16 < 8
        own = [eown[pl.ds(at, chunk), i] for i in range(4)]
        la, lb = from_l[pl.ds(at, chunk), 0], from_l[pl.ds(at, chunk), 1]
        ra, rb = from_r[pl.ds(at, chunk), 0], from_r[pl.ds(at, chunk), 1]

        def assemble(i, from_left, from_right):
            return join(jnp.where(low, from_left, own[i]), jnp.where(low, own[i], from_right))

        c0 = assemble(0, la, ra)
        c1 = assemble(1, pltpu.roll(la, LON - 8, 2), pltpu.roll(ra, 8, 2))
        uu = assemble(2, lb, rb)
        vv = assemble(3, pltpu.roll(lb, LON - 8, 2), pltpu.roll(rb, 8, 2))
        done = upwind(c0, c1, uu, vv, level_mask(0, k, 0, 0), level_mask(1, k, 0, 0), strip_shifts())
        for n in range(2):
            both = done[n].reshape(chunk, 2, 8, LON)
            g = gwin[n, pl.ds(at, chunk)]
            awin[pl.ds(at, chunk), n, 0] = jnp.where(low, pltpu.roll(both[:, 0], LON - 4, 2), g)
            awin[pl.ds(at, chunk), n, 1] = jnp.where(low, g, pltpu.roll(both[:, 1], 4, 2))
        return carry

    strip_transport(0, 0)
    for copy in lon_2:
        copy.wait_recv()
    for i in range(2):
        guest_l = guest_r = None
        for j in range(3):
            span = pl.ds(2 + j * guests, guests)
            part_l = pltpu.roll(from_l[span, i], 2 + 2 * j, 2)
            part_r = pltpu.roll(from_r[span, i], LON - 6 + 2 * j, 2)
            guest_l = part_l if j == 0 else jnp.where(slot >= 2 + 2 * j, part_l, guest_l)
            guest_r = part_r if j == 0 else jnp.where(slot >= 2 * j, part_r, guest_r)
        from_l[pl.ds(2 + hosts, guests), i] = guest_l
        from_r[pl.ds(2 + hosts, guests), i] = guest_r

    strip_transport(1, 0)

    @pl.when(has_dn)
    def _():
        ups[4].wait_recv()
        ups[6].wait_recv()

    @pl.when(has_up)
    def _():
        downs[4].wait_recv()
        downs[5].wait_recv()

    lax.fori_loop(0, 2, flux_ends, 0)

    low2 = lanes((2, 8, LON)) % 16 < 8
    for at in (0, n_lev + 2):
        pack_windows(at, 2)
        for n in range(2):
            g = gwin[n, pl.ds(at, 2)]
            awin[pl.ds(at, 2), n, 0] = jnp.where(low2, awin[pl.ds(at, 2), n, 0], g)
            awin[pl.ds(at, 2), n, 1] = jnp.where(low2, g, awin[pl.ds(at, 2), n, 1])

    @pl.when(inner)
    def _():
        z_copy.wait_recv()
        z = zmat[...]
        inv_t = 1.0 / (1.0 - z * send_end[o_end, o_end])
        tmat[0] = inv_t
        beta = z * send_end[i_end, o_end] * inv_t
        tmat[1] = beta
        qmat[...] = send_end[i_end, i_end] + send_end[o_end, i_end] * beta
        q_copy.start()


    chunk = FC
    shape = (chunk, 8, LON)
    flatshape = (2 * chunk, 8, LON)

    def strip_flux(step, carry):
        at = step * chunk
        k = first + at - 1
        wl = lanes(shape) % 16
        lb, rb = from_l[pl.ds(at + 1, chunk), 1], from_r[pl.ds(at + 1, chunk), 1]
        kl = jnp.where(wl == 3, pltpu.roll(lb, LON - 7, 2), kown[pl.ds(at, chunk), 0])
        kr = jnp.where(wl == 12, pltpu.roll(rb, 7, 2), kown[pl.ds(at, chunk), 1])
        kappa = jnp.where(level_mask(2, k, 0, 0), 0.25 * join(kl, kr), 0.0)

        def window(shift):
            return [awin[pl.ds(at + shift, chunk), n].reshape(flatshape) for n in range(2)]

        _, _, north, south = strip_shifts()
        mid = window(1)
        f, y, w = fluxes(
            window(0), mid, window(2), [north(c) for c in mid], [south(c) for c in mid], kappa,
            level_mask(3, k, 0, 0), level_mask(4, k, 0, 0), level_mask(2, k, 1, 1),
        )
        for n in range(2):
            sflat[pl.ds(at, chunk), n] = (f[n] + (north(y[n]) - south(y[n]))).reshape(chunk, 2, 8, LON)
            svert[pl.ds(at, chunk), n] = w[n].reshape(chunk, 2, 8, LON)
        return carry

    lax.fori_loop(0, (n_lev + 4) // chunk, strip_flux, 0)

    chunk = n_lev
    shape = (chunk, 8, LON)
    flatshape = (2 * chunk, 8, LON)

    def strip_update(step, carry):
        at = step * chunk
        low = lanes(shape) % 16 < 8
        wet = level_mask(2, first + at, 0, 0)
        for n in range(2):
            gain = (
                sflat[pl.ds(at + 1, chunk), n] + svert[pl.ds(at + 2, chunk), n] - svert[pl.ds(at, chunk), n]
            ).reshape(flatshape)
            new = awin[pl.ds(at + 2, chunk), n].reshape(flatshape) + jnp.where(wet, gain, 0.0)
            both = new.reshape(chunk, 2, 8, LON)
            edge[pl.ds(at, chunk), n] = jnp.where(
                low, pltpu.roll(both[:, 1], LON - 4, 2), pltpu.roll(both[:, 0], 4, 2)
            )
        return carry

    lax.fori_loop(0, n_lev // chunk, strip_update, 0)

    yend[...] = jnp.zeros(yend.shape, jnp.float32)
    fval[0] = jnp.zeros((2,) + plane, jnp.float32)
    lane = lanes(plane)
    on_edge = (lane < 6) | (lane >= LON - 6)

    group = 10

    def way_down(n, step, carry):
        at = step * group
        value, total = fval[at, n], yend[0, n]
        for i in range(group):
            here = at + i
            wet = bmask[0] > first + here
            new = adv[here + 2, n] + jnp.where(wet, flat[here + 1, n] + vert[here + 2, n] - vert[here, n], 0.0)
            packed = edge[here, n]
            fixed = jnp.concatenate(
                [pltpu.roll(packed, (LON - 8 - 16 * g) % LON, 1) for g in range(8)], axis=0
            )
            new = jnp.where(on_edge, fixed, new)
            value = new * inv[here] + gdn[here] * value
            fval[here + 1, n] = value
            total = total + rprod[here] * value
        yend[0, n] = total
        return carry

    z_val = [remote(yend.at[i_end, n], zval.at[n], ZV + n, (lon, in_dev)) for n in range(2)]
    y_val = [remote(yval.at[n], ypart.at[n], YV + n, (lon, 3 - dep)) for n in range(2)]
    x_val = [remote(xout.at[n], xend.at[i_end, n], XO + n, (lon, out_dev)) for n in range(2)]

    for n in range(2):
        lax.fori_loop(0, n_lev // group, functools.partial(way_down, n), 0)
        yend[1, n] = fval[n_lev, n]

        @pl.when(outer)
        def _():
            z_val[n].start()

    @pl.when(outer)
    def _():
        xend[o_end] = jnp.zeros((2,) + plane, jnp.float32)

    @pl.when(inner)
    def _():
        for n in range(2):
            z_val[n].wait_recv()
            alpha = (zval[n] + zmat[...] * yend[o_end, n]) * tmat[0]
            xend[o_end, n] = alpha
            yval[n] = yend[i_end, n] + send_end[o_end, i_end] * alpha
            y_val[n].start()

    def back_matrix(step, carry):
        p_low, q_low = carry
        at = n_lev - 1 - step
        ratio = rdn[at]
        p = pspk[at] + ratio * p_low
        q = ratio * q_low
        pspk[at] = p
        qspk[at] = q
        return p, q

    lax.fori_loop(0, n_lev, back_matrix, (zero, one))

    def way_up(step, carry):
        at = n_lev - 1 - step
        ratio = rdn[at - 1]
        for n in range(2):
            fval[at, n] = fval[at, n] + ratio * fval[at + 1, n]
        return carry

    lax.fori_loop(0, n_lev - 1, way_up, 0)

    @pl.when(inner)
    def _():
        q_copy.wait_recv()
        q_other = qpart[...]
        inv_m = 1.0 / (1.0 - q_other * qmat[...])
        for n in range(2):
            y_val[n].wait_recv()
            x_in = (ypart[n] + q_other * yval[n]) * inv_m
            xout[n] = (yend[o_end, n] + send_end[o_end, o_end] * zval[n] + send_end[i_end, o_end] * x_in) * tmat[0]
            x_val[n].start()
            xend[i_end, n] = x_in
            xend[o_end, n] = xend[o_end, n] + tmat[1] * x_in

    @pl.when(outer)
    def _():
        for copy in x_val:
            copy.wait_recv()

    part = n_lev // 4
    for i in range(4):
        def finish(at, carry):
            p, q = pspk[at], qspk[at]
            for n in range(2):
                out_hbm[n, at] = fval[at + 1, n] + p * xend[0, n] + q * xend[1, n]
            return carry

        lax.fori_loop(i * part, (i + 1) * part, finish, 0)

    for copy in lon_1 + lon_2 + [bot_r, bot_l]:
        copy.wait_send()

    @pl.when(has_up)
    def _():
        for copy in ups:
            copy.wait_send()

    @pl.when(has_dn)
    def _():
        for copy in downs:
            copy.wait_send()

    @pl.when(outer)
    def _():
        z_copy.wait_send()
        for copy in z_val:
            copy.wait_send()

    @pl.when(inner)
    def _():
        q_copy.wait_send()
        for copy in y_val + x_val:
            copy.wait_send()


def per_device(n_lon, n_dep, tracers, u_east, v_north, kappa_h, kappa_v, bottom):
    n_lev = tracers.shape[1]
    ext = n_lev + 4

    def f32(*shape):
        return pltpu.VMEM(shape, jnp.float32)

    def i32(*shape):
        return pltpu.VMEM(shape, jnp.int32)

    scratch = [
        f32(2, n_lev, LAT, LON), f32(n_lev, LAT, LON), f32(n_lev, LAT, LON),
        f32(n_lev + 2, LAT, LON), f32(n_lev + 1, LAT, LON), i32(LAT, LON),
        i32(5, LAT, LON), i32(5, 2, 8, LON), i32(3, 8, LON), i32(2, 8, LON),
        f32(ext, 4, 8, LON), f32(ext, 2, 8, LON),
        f32(n_lev, 2, 8, LON), f32(n_lev, 2, 8, LON),
        f32(ext + 1, 2, 8, LON), f32(ext + 1, 2, 8, LON),
        f32(ext, 2, LAT, LON), f32(n_lev + 2, 2, LAT, LON), f32(n_lev + 2, 2, LAT, LON),
        f32(2, ext, 8, LON), f32(ext + 2, 2, 2, 8, LON),
        f32(ext, 2, 2, 8, LON), f32(ext, 2, 2, 8, LON), f32(n_lev, 2, 8, LON),
    ]
    scratch += [f32(n_lev, LAT, LON)] * 6
    scratch += [
        f32(n_lev + 1, 2, LAT, LON), f32(2, 2, LAT, LON), f32(2, 2, LAT, LON),
        f32(LAT, LON), f32(LAT, LON), f32(LAT, LON),
        f32(2, LAT, LON), f32(2, LAT, LON), f32(2, LAT, LON), f32(2, LAT, LON),
        f32(2, 2, LAT, LON), f32(2, LAT, LON),
        pltpu.SemaphoreType.DMA((4 * NQ + 2,)),
        pltpu.SemaphoreType.DMA((N_COPIES,)), pltpu.SemaphoreType.DMA((N_COPIES,)),
    ]
    hbm = pl.BlockSpec(memory_space=pltpu.HBM)
    return pl.pallas_call(
        functools.partial(kernel, n_lon, n_dep, n_lev),
        out_shape=jax.ShapeDtypeStruct(tracers.shape, jnp.float32),
        in_specs=[hbm] * 6,
        out_specs=pl.BlockSpec(memory_space=pltpu.VMEM),
        scratch_shapes=scratch,
        name="tracer_step",
        compiler_params=pltpu.CompilerParams(
            collective_id=0, has_side_effects=True, vmem_limit_bytes=48 << 20
        ),
    )(*(pltpu.with_memory_space_constraint(a, pltpu.HBM) for a in (tracers, u_east, v_north, kappa_h, kappa_v, bottom)))


def solution(mesh):
    n_lon, n_dep = mesh.shape["lon"], mesh.shape["dep"]
    level = P("dep", None, "lon")
    return jax.shard_map(
        functools.partial(per_device, n_lon, n_dep),
        mesh=mesh,
        in_specs=(P(None, "dep", None, "lon"), level, level, level, level, P(None, "lon")),
        out_specs=P(None, "dep", None, "lon"),
        check_vma=False,
    )
```
